256 devices in a mesh: samp: 4 (over z_hi, core), vert: 64 (over x, z_lo, y).
Axes of the slice: x: 4, y: 4, z: 8 (z_hi: 2, z_lo: 4; z = z_hi * 4 + z_lo), core: 2. Of those that a mesh axis runs over, the one named last changes fastest.
Arguments:
- inputs: bfloat16 [8, 262144, 128], P('samp', 'vert'), may hold values from -6 to 6
- cotangent: bfloat16 [8, 262144, 128], P('samp', 'vert'), may hold values from -6 to 6
- basis: bfloat16 [262144, 1024], P('vert'), may hold values from -0.0234375 to 0.0234375
- mode_weights: bfloat16 [1024, 128, 128], P('vert'), may hold values from -0.5 to 0.5
- w_up: bfloat16 [128, 512], replicated, may hold values from -0.5 to 0.5
- b_up: float32 [512], replicated, may hold values from -4 to 4
- w_down: bfloat16 [512, 128], replicated, may hold values from -0.25 to 0.25
Outputs:
- grad_input: bfloat16 [8, 262144, 128], P('samp', 'vert')
- grad_modes: float32 [1024, 128, 128], P('vert')
- grad_w_up: float32 [128, 512], replicated
- grad_b_up: float32 [512], replicated
- grad_w_down: float32 [512, 128], replicated
The draws below stay inside these ranges and needn't reach their ends.
All inputs are finite; a program needn't handle non-finite values.
Results may differ from the reference program's by a relative error of at most 0.0055.
Values may be sent and summed in bfloat16 or wider, within the bound.
No kernel may reach another device: no remote copies, remote signals or barrier semaphores. Data moves between devices by JAX's collectives and lax.ppermute only.
A program may use at most 128 MiB of HBM per device.

```python
import jax
import jax.numpy as jnp
from jax import lax

C = 128
H = 512
K = 1024
VERTICES = 262144
SAMPLES = 8


def shard_levels(stream_key, extent, pieces, smallest, top_value):
    level, own = 1.0, jax.random.fold_in(stream_key, 6)
    for axis_at, blocks in pieces:
        steps = jnp.exp(jax.random.uniform(jax.random.fold_in(own, axis_at), (blocks,), jnp.float32, smallest / len(pieces), top_value / len(pieces)))
        level = level * jnp.repeat(steps, extent[axis_at] // blocks).reshape([-1 if axis == axis_at else 1 for axis in range(len(extent))])
    return level


def normal_values(own_key, dims, scale, most, shards=(), held_as=jnp.bfloat16):
    loudness = shard_levels(own_key, dims, shards, -0.22, 0.18) if shards else 1.0
    entries = jax.random.normal(own_key, dims, jnp.float32) * scale * loudness
    return jnp.minimum(jnp.maximum(entries, -most), most).astype(held_as)


def setup_inputs(seed: int = 0) -> dict:
    seeds = jax.random.split(jax.random.key(seed), 8)
    return {
        "inputs": normal_values(seeds[0], (SAMPLES, VERTICES, C), 1.0, 6.0, ((0, 4), (1, 64))),
        "cotangent": normal_values(seeds[1], (SAMPLES, VERTICES, C), 1.0, 6.0, ((0, 4), (1, 64))),
        "basis": normal_values(seeds[2], (VERTICES, K), (VERTICES // 4) ** -0.5, 0.0234375, ((0, 64),)),
        "mode_weights": normal_values(seeds[3], (K, C, C), C ** -0.5, 0.5, ((0, 64),)),
        "w_up": normal_values(seeds[4], (C, H), C ** -0.5, 0.5),
        "b_up": normal_values(seeds[5], (H,), 1.0, 4.0, (), jnp.float32),
        "w_down": normal_values(seeds[6], (H, C), H ** -0.5, 0.25),
    }


def gelu_value(pre_act):
    inner = 0.7978845608 * (pre_act + 0.044715 * pre_act * pre_act * pre_act)
    return 0.5 * pre_act * (1.0 + jnp.tanh(inner))


def gelu_slope(pre_act):
    inner = 0.7978845608 * (pre_act + 0.044715 * pre_act * pre_act * pre_act)
    tangent = jnp.tanh(inner)
    return 0.5 * (1.0 + tangent) + 0.5 * pre_act * (1.0 - tangent * tangent) * 0.7978845608 * (1.0 + 3.0 * 0.044715 * pre_act * pre_act)


def reference(inputs, cotangent, basis, mode_weights, w_up, b_up, w_down):
    mixing = mode_weights.astype(jnp.float32)
    grad_modes = jnp.zeros((K, C, C), jnp.float32)
    grad_w_up = jnp.zeros((C, H), jnp.float32)
    grad_b_up = jnp.zeros((H,), jnp.float32)
    grad_w_down = jnp.zeros((H, C), jnp.float32)
    results = []
    for sample in range(SAMPLES):
        coeffs = jnp.dot(basis.T, inputs[sample], preferred_element_type=jnp.float32)
        grad_out = jnp.dot(basis.T, cotangent[sample], preferred_element_type=jnp.float32)
        grad_coef = jnp.einsum("kd,kcd->kc", grad_out, mixing, precision=lax.Precision.HIGHEST).astype(jnp.bfloat16)
        grad_modes = grad_modes + jnp.einsum("kc,kd->kcd", coeffs, grad_out, precision=lax.Precision.HIGHEST)
        spectral = jnp.dot(basis, grad_coef, preferred_element_type=jnp.float32)
        pre_act = jnp.dot(inputs[sample], w_up, preferred_element_type=jnp.float32) + b_up
        hidden = gelu_value(pre_act).astype(jnp.bfloat16)
        grad_hidden = jnp.dot(cotangent[sample], w_down.T, preferred_element_type=jnp.float32)
        grad_pre = (grad_hidden * gelu_slope(pre_act)).astype(jnp.bfloat16)
        pointwise = jnp.dot(grad_pre, w_up.T, preferred_element_type=jnp.float32)
        results.append((spectral + pointwise).astype(jnp.bfloat16))
        grad_w_up = grad_w_up + jnp.dot(inputs[sample].T, grad_pre, preferred_element_type=jnp.float32)
        grad_b_up = grad_b_up + jnp.sum(grad_pre.astype(jnp.float32), axis=0)
        grad_w_down = grad_w_down + jnp.dot(hidden.T, cotangent[sample], preferred_element_type=jnp.float32)
    grad_input = jnp.stack(results, axis=0)
    return (grad_input, grad_modes, grad_w_up, grad_b_up, grad_w_down)
```

```python
import functools

import jax
import jax.numpy as jnp
from jax import lax
from jax.experimental import pallas as pl
from jax.experimental.pallas import tpu as pltpu
from jax.sharding import Mesh
from jax.sharding import PartitionSpec as P

F32 = jnp.float32
BF16 = jnp.bfloat16
ROOT = 0.7978845608
CUBE = 0.044715
RING = 4
OWNED = 16
SAMP = ("zhi", "core")
VERT = ("x", "zlo", "y")


def product(a, b, a_dim, b_dim):
    return lax.dot_general(a, b, (((a_dim,), (b_dim,)), ((), ())), preferred_element_type=F32)


def project_body(block_ref, basis_ref, inputs_ref, cotangent_ref, out_ref, total, *, last):
    step = pl.program_id(0)

    @pl.when(step == 0)
    def _():
        total[...] = jnp.zeros_like(total)

    fields = jnp.concatenate(
        [inputs_ref[0], cotangent_ref[0], inputs_ref[1], cotangent_ref[1]], axis=1
    )
    total[...] += product(basis_ref[...], fields, 0, 0)

    @pl.when(step == last)
    def _():
        out_ref[...] = total[...].astype(out_ref.dtype)


def project(block, basis, inputs, cotangent, dtype, rows=2048, width=256):
    steps = basis.shape[0] // rows
    field = pl.BlockSpec((2, rows, 128), lambda i, b: (0, i, 0))
    return pl.pallas_call(
        functools.partial(project_body, last=steps - 1),
        grid_spec=pltpu.PrefetchScalarGridSpec(
            num_scalar_prefetch=1,
            grid=(steps,),
            in_specs=[pl.BlockSpec((rows, width), lambda i, b: (i, b[0])), field, field],
            out_specs=pl.BlockSpec((width, 512), lambda i, b: (0, 0)),
            scratch_shapes=[pltpu.VMEM((width, 512), F32)],
        ),
        out_shape=jax.ShapeDtypeStruct((width, 512), dtype),
        compiler_params=pltpu.CompilerParams(vmem_limit_bytes=20 << 20),
        cost_estimate=pl.CostEstimate(
            flops=2 * 4096 * width * 512, bytes_accessed=8 << 20, transcendentals=0
        ),
        name="project",
    )(block, basis, inputs, cotangent)


def pointwise_body(
    x_ref, c_ref, up_ref, bias_ref, down_ref, _p, gu_in, gd_in, gb_in, p_ref, gu_ref, gd_ref, gb_ref
):
    @pl.when(pl.program_id(0) == 0)
    def _():
        gu_ref[...] = gu_in[...]
        gd_ref[...] = gd_in[...]
        gb_ref[...] = gb_in[...]

    up, down = up_ref[...], down_ref[...]
    x, c = x_ref[...], c_ref[...]
    z = product(x, up, 1, 0) + bias_ref[...]
    square = z * z
    t = jnp.tanh(z * (ROOT + (ROOT * CUBE) * square))
    half = 0.5 * z
    plus = 1.0 + t
    hidden = (half * plus).astype(BF16)
    slope = 0.5 * plus + half * (1.0 - t * t) * (ROOT + (3.0 * CUBE * ROOT) * square)
    grad_pre = (product(c, down, 1, 1) * slope).astype(BF16)
    p_ref[...] = product(grad_pre, up, 1, 1)
    with_ones = jnp.concatenate([x, jnp.ones((x.shape[0], 128), BF16)], axis=1)
    sums = product(with_ones, grad_pre, 0, 0)
    gu_ref[...] += sums[:128]
    gb_ref[...] += sums[128:136]
    gd_ref[...] += product(c, hidden, 0, 0)


def pointwise(first, count, x, c, up, bias, down, carried, rows=1024):
    def fixed(shape):
        return pl.BlockSpec(shape, lambda i: (0, 0))

    def moving():
        return pl.BlockSpec((rows, 128), lambda i: (first + i, 0))

    acc = [fixed((128, 512)), fixed((128, 512)), fixed((8, 512))]
    return pl.pallas_call(
        pointwise_body,
        grid=(count,),
        in_specs=[
            moving(), moving(), fixed((128, 512)), fixed((1, 512)), fixed((512, 128)),
            pl.BlockSpec(memory_space=pl.ANY), *acc,
        ],
        out_specs=[moving(), *acc],
        out_shape=[jax.ShapeDtypeStruct(v.shape, v.dtype) for v in carried],
        input_output_aliases={5: 0},
        compiler_params=pltpu.CompilerParams(vmem_limit_bytes=28 << 20),
        cost_estimate=pl.CostEstimate(
            flops=10 * count * rows * 128 * 512,
            bytes_accessed=count * rows * 128 * 8,
            transcendentals=count * rows * 512,
        ),
        name="pointwise",
    )(x, c, up, bias, down, *carried)


def finish_body(order_ref, b0, b1, b2, b3, g0, g1, g2, g3, p_ref, out_ref):
    total = product(b0[...], g0[...], 1, 0) + product(b1[...], g1[...], 1, 0)
    total += product(b2[...], g2[...], 1, 0) + product(b3[...], g3[...], 1, 0)
    out_ref[0] = (total[:, :128] + p_ref[0]).astype(out_ref.dtype)
    out_ref[1] = (total[:, 128:] + p_ref[1]).astype(out_ref.dtype)


def finish(order, basis, parts, point, rows=1024):
    vertices = basis.shape[0]

    def column(j):
        return pl.BlockSpec((rows, 256), lambda i, o: (i, o[j]))

    both = pl.BlockSpec((2, rows, 128), lambda i, o: (0, i, 0))
    return pl.pallas_call(
        finish_body,
        grid_spec=pltpu.PrefetchScalarGridSpec(
            num_scalar_prefetch=1,
            grid=(vertices // rows,),
            in_specs=[column(j) for j in range(RING)]
            + [pl.BlockSpec((256, 256), lambda i, o: (0, 0))] * RING
            + [both],
            out_specs=both,
        ),
        out_shape=jax.ShapeDtypeStruct((2, vertices, 128), BF16),
        compiler_params=pltpu.CompilerParams(vmem_limit_bytes=24 << 20),
        cost_estimate=pl.CostEstimate(
            flops=2 * vertices * 1024 * 256, bytes_accessed=16 << 20, transcendentals=0
        ),
        name="finish",
    )(order, basis, basis, basis, basis, *parts, point)


def send(value, axis, shift):
    return lax.ppermute(value, axis, [(i, (i + shift) % RING) for i in range(RING)])


def take(stacked, index, axis=0):
    return lax.dynamic_index_in_dim(stacked, index % RING, axis, keepdims=False)


def reduce_stage(total, axis, dim):
    me = lax.axis_index(axis)
    arrived = [send(take(total, me + s, dim).astype(BF16), axis, s) for s in (2, 1, 3)]
    own = take(total, me, dim)
    for part in arrived:
        own = own + part.astype(F32)
    return own


def gather_stage(value, axis, dim):
    me = lax.axis_index(axis)
    arrived = [(0, value)] + [(s, send(value, axis, s)) for s in (2, 1, 3)]
    shape = value.shape[:dim] + (RING,) + value.shape[dim:]
    out = jnp.zeros(shape, value.dtype)
    for s, part in arrived:
        out = lax.dynamic_update_index_in_dim(out, part, (me - s + RING) % RING, dim)
    return out


def exchange_samp(value):
    me = lax.axis_index("zhi") * 2 + lax.axis_index("core")
    pairs = {
        1: lax.ppermute(value, "core", [(0, 1), (1, 0)]),
        2: lax.ppermute(value, "zhi", [(0, 1), (1, 0)]),
        3: lax.ppermute(value, SAMP, [(i, 3 - i) for i in range(RING)]),
    }
    out = jnp.zeros((RING,) + value.shape, value.dtype)
    out = lax.dynamic_update_index_in_dim(out, value, me, 0)
    for flip, part in pairs.items():
        out = lax.dynamic_update_index_in_dim(out, part, me ^ flip, 0)
    return out


def weight_sums(gu, gd, gb):
    def rows(v):
        return v.reshape(-1, RING, 128).swapaxes(0, 1)

    body = jnp.concatenate([rows(gu), rows(gd)], axis=1)
    bias = jnp.pad(gb[:1].reshape(RING, 128), ((0, 12), (0, 0)))
    for axis in ("x", "y", "zlo"):
        if axis != "x":
            body = body.reshape(RING, -1, 128)
        me = lax.axis_index(axis)
        arrived = []
        for s in (2, 1, 3):
            message = jnp.concatenate([take(body, me + s), bias], axis=0).astype(BF16)
            arrived.append(send(message, axis, s).astype(F32))
        body = take(body, me)
        for part in arrived:
            body = body + part[:-16]
            bias = bias + part[-16:]
    both = exchange_samp(jnp.concatenate([body, bias], axis=0).astype(BF16)).astype(F32)
    both = (both[0] + both[1]) + (both[2] + both[3])
    bias = both[-16:][:RING].reshape(512)
    body = both[:-16].astype(BF16)
    for axis in ("zlo", "y", "x"):
        body = gather_stage(body, axis, 0)
        if axis != "x":
            body = body.reshape(-1, 128)
    body = body.astype(F32).swapaxes(0, 1).reshape(-1, 512)
    return body[:128], bias, body[128:].T


def per_device(inputs, cotangent, basis, mode_weights, w_up, b_up, w_down):
    x_at = lax.axis_index("x")
    vertices = inputs.shape[1]

    arrived = []
    for s in (2, 1, 3):
        block = ((x_at + s) % RING).reshape(1)
        arrived.append(send(project(block, basis, inputs, cotangent, BF16), "x", s))
    own = project(x_at.reshape(1), basis, inputs, cotangent, F32)

    flat_x = inputs.reshape(-1, 128)
    flat_c = cotangent.reshape(-1, 128)
    carried = [
        jnp.zeros((2 * vertices, 128), F32),
        jnp.zeros((128, 512), F32),
        jnp.zeros((128, 512), F32),
        jnp.zeros((8, 512), F32),
    ]
    bias = b_up.reshape(1, 512)
    first = 0
    for count in (3, 2, 2, 1):
        carried = pointwise(first, count, flat_x, flat_c, w_up, bias, w_down, carried)
        first += count
    point, gu, gd, gb = carried

    for part in arrived:
        own = own + part.astype(F32)
    own = reduce_stage(own.reshape(RING, RING, OWNED, 512), "y", 1)
    own = reduce_stage(own, "zlo", 0)

    grad_out = jnp.stack([own[:, 128:256], own[:, 384:]], axis=1)
    grad_coef = jnp.einsum(
        "ksd,kcd->ksc", grad_out, mode_weights.astype(F32), precision=lax.Precision.HIGHEST
    ).astype(BF16).reshape(OWNED, 256)
    coef = gather_stage(grad_coef, "zlo", 0)
    coef = gather_stage(coef, "y", 1).reshape(256, 256)
    parts = [coef] + [send(coef, "x", s) for s in (1, 2, 3)]
    order = jnp.stack([(x_at - s + RING) % RING for s in range(RING)]).astype(jnp.int32)
    grad_input = finish(order, basis, parts, point.reshape(2, vertices, 128))

    everyone = exchange_samp(own).reshape(RING, OWNED, 2, 2, 128)
    grad_modes = jnp.einsum(
        "gksc,gksd->kcd", everyone[:, :, :, 0], everyone[:, :, :, 1],
        precision=lax.Precision.HIGHEST,
    )
    grad_w_up, grad_b_up, grad_w_down = weight_sums(gu, gd, gb)
    return (grad_input, grad_modes, grad_w_up, grad_b_up, grad_w_down)


def solution(mesh):
    fine = Mesh(mesh.devices.reshape(2, 2, RING, RING, RING), SAMP + VERT)
    in_specs = (
        P(SAMP, VERT, None),
        P(SAMP, VERT, None),
        P(VERT, None),
        P(VERT, None, None),
        P(),
        P(),
        P(),
    )
    out_specs = (P(SAMP, VERT, None), P(VERT, None, None), P(), P(), P())
    return jax.shard_map(
        per_device, mesh=fine, in_specs=in_specs, out_specs=out_specs, check_vma=False
    )
```

```python
import functools

import jax
import jax.numpy as jnp
from jax import lax
from jax.experimental import pallas as pl
from jax.experimental.pallas import tpu as pltpu
from jax.sharding import Mesh
from jax.sharding import PartitionSpec as P

F32 = jnp.float32
BF16 = jnp.bfloat16
ROOT = 0.7978845608
CUBE = 0.044715
RING = 4
OWNED = 16
SAMP = ("zhi", "core")
VERT = ("x", "zlo", "y")
MIB = 1 << 20


def product(a, b, a_dim, b_dim):
    return lax.dot_general(a, b, (((a_dim,), (b_dim,)), ((), ())), preferred_element_type=F32)


def whole(shape):
    return pl.BlockSpec(shape, lambda *_: (0,) * len(shape))


def project_body(x_at, basis_ref, inputs_ref, cotangent_ref, one, two, three, own, total):
    step = pl.program_id(0)

    @pl.when(step == 0)
    def _():
        total[...] = jnp.zeros_like(total)

    fields = jnp.concatenate(
        [inputs_ref[0], cotangent_ref[0], inputs_ref[1], cotangent_ref[1]], axis=1
    )
    total[...] += product(basis_ref[...], fields, 0, 0)

    @pl.when(step == pl.num_programs(0) - 1)
    def _():
        for shift, out in enumerate((own, one, two, three)):
            first = pl.multiple_of(lax.rem(x_at[0] + shift, RING) * 256, 256)
            out[...] = total[pl.ds(first, 256), :].astype(out.dtype)


def project(x_at, basis, inputs, cotangent, rows=1024):
    field = pl.BlockSpec((2, rows, 128), lambda i, b: (0, i, 0))
    return pl.pallas_call(
        project_body,
        grid_spec=pltpu.PrefetchScalarGridSpec(
            num_scalar_prefetch=1,
            grid=(basis.shape[0] // rows,),
            in_specs=[pl.BlockSpec((rows, 1024), lambda i, b: (i, 0)), field, field],
            out_specs=[whole((256, 512))] * 4,
            scratch_shapes=[pltpu.VMEM((1024, 512), F32)],
        ),
        out_shape=[jax.ShapeDtypeStruct((256, 512), BF16)] * 3
        + [jax.ShapeDtypeStruct((256, 512), F32)],
        compiler_params=pltpu.CompilerParams(vmem_limit_bytes=56 * MIB),
        cost_estimate=pl.CostEstimate(
            flops=2 * 4096 * 1024 * 512, bytes_accessed=13 * MIB, transcendentals=0
        ),
        name="project",
    )(x_at, basis, inputs, cotangent)


def pointwise_body(x_ref, c_ref, up_ref, bias_ref, down_ref, p_ref, gu_ref, gd_ref, gb_ref):
    @pl.when(pl.program_id(0) == 0)
    def _():
        gu_ref[...] = jnp.zeros_like(gu_ref)
        gd_ref[...] = jnp.zeros_like(gd_ref)
        gb_ref[...] = jnp.zeros_like(gb_ref)

    up, down = up_ref[...], down_ref[...]
    x, c = x_ref[...], c_ref[...]
    z = product(x, up, 1, 0) + bias_ref[...]
    square = z * z
    t = jnp.tanh(z * (ROOT + (ROOT * CUBE) * square))
    half = 0.5 * z
    plus = 1.0 + t
    hidden = (half * plus).astype(BF16)
    slope = 0.5 * plus + half * (1.0 - t * t) * (ROOT + (3.0 * CUBE * ROOT) * square)
    grad_pre = (product(c, down, 1, 1) * slope).astype(BF16)
    p_ref[...] = product(grad_pre, up, 1, 1)
    with_ones = jnp.concatenate([x, jnp.ones((x.shape[0], 128), BF16)], axis=1)
    sums = product(with_ones, grad_pre, 0, 0)
    gu_ref[...] += sums[:128]
    gb_ref[...] += sums[128:136]
    gd_ref[...] += product(c, hidden, 0, 0)


def pointwise(x, c, up, bias, down, rows=1024):
    count = x.shape[0] // rows
    moving = pl.BlockSpec((rows, 128), lambda i: (i, 0))
    sums = [(128, 512), (128, 512), (8, 512)]
    return pl.pallas_call(
        pointwise_body,
        grid=(count,),
        in_specs=[moving, moving, whole((128, 512)), whole((1, 512)), whole((512, 128))],
        out_specs=[moving] + [whole(s) for s in sums],
        out_shape=[jax.ShapeDtypeStruct(s, F32) for s in [x.shape] + sums],
        compiler_params=pltpu.CompilerParams(vmem_limit_bytes=52 * MIB),
        cost_estimate=pl.CostEstimate(
            flops=10 * count * rows * 128 * 512,
            bytes_accessed=count * rows * 128 * 8,
            transcendentals=count * rows * 512,
        ),
        name="pointwise",
    )(x, c, up, bias, down)


def pack_body(own, one, two, three, gu, gd, gb, out):
    total = own[...] + one[...].astype(F32) + two[...].astype(F32) + three[...].astype(F32)
    row = lax.broadcasted_iota(jnp.int32, (8, 128), 0)
    bias = jnp.zeros((8, 128), F32)
    for g in range(4):
        bias = jnp.where(row == g, gb[:, g * 128 : (g + 1) * 128], bias)
    bias = jnp.concatenate([bias, jnp.zeros((8, 128), F32)], axis=0).astype(BF16)
    for j in range(16):
        for g in range(4):
            out[j, g * 16 : (g + 1) * 16, :] = total[
                j * 16 : (j + 1) * 16, g * 128 : (g + 1) * 128
            ].astype(BF16)
        for k, ref in enumerate((gu, gd)):
            for q in range(2):
                pair = [
                    ref[j * 8 : (j + 1) * 8, g * 128 : (g + 1) * 128] for g in (2 * q, 2 * q + 1)
                ]
                first = 64 + k * 32 + q * 16
                out[j, first : first + 16, :] = jnp.concatenate(pair, axis=0).astype(BF16)
        out[j, 128:144, :] = bias


def small(body, name, out_shape, *args):
    return pl.pallas_call(
        body,
        out_shape=out_shape,
        compiler_params=pltpu.CompilerParams(vmem_limit_bytes=32 * MIB),
        name=name,
    )(*args)


def own_body(messages, weights, sums_ref, coef_ref):
    sums = messages[0].astype(F32)
    for j in range(1, 16):
        sums = sums + messages[j].astype(F32)
    sums_ref[...] = sums
    parts = []
    for sample in range(2):
        rest = sums[sample * 32 + 16 : sample * 32 + 32]
        for _ in range(3):
            parts.append(rest.astype(BF16))
            rest = rest - parts[-1].astype(F32)
    left = jnp.concatenate(parts, axis=0)
    row = lax.broadcasted_iota(jnp.int32, (16, 128), 0)
    first = jnp.zeros((16, 128), F32)
    second = jnp.zeros((16, 128), F32)
    for k in range(16):
        mixed = product(left, weights[k], 1, 1)
        first = jnp.where(row == k, mixed[0:16] + mixed[16:32] + mixed[32:48], first)
        second = jnp.where(row == k, mixed[48:64] + mixed[64:80] + mixed[80:96], second)
    coef = jnp.concatenate([first, second], axis=1).astype(BF16)
    for v in range(64):
        coef_ref[v] = coef


def finish_body(basis_ref, coef_ref, p_ref, out_ref):
    total = product(basis_ref[...], coef_ref[...], 1, 0)
    out_ref[0] = (total[:, :128] + p_ref[0]).astype(out_ref.dtype)
    out_ref[1] = (total[:, 128:] + p_ref[1]).astype(out_ref.dtype)


def finish(basis, coef, point, rows=1024):
    vertices = basis.shape[0]
    both = pl.BlockSpec((2, rows, 128), lambda i: (0, i, 0))
    return pl.pallas_call(
        finish_body,
        grid=(vertices // rows,),
        in_specs=[pl.BlockSpec((rows, 1024), lambda i: (i, 0)), whole((1024, 256)), both],
        out_specs=both,
        out_shape=jax.ShapeDtypeStruct((2, vertices, 128), BF16),
        compiler_params=pltpu.CompilerParams(vmem_limit_bytes=56 * MIB),
        cost_estimate=pl.CostEstimate(
            flops=2 * vertices * 1024 * 256, bytes_accessed=16 * MIB, transcendentals=0
        ),
        name="finish",
    )(basis, coef, point)


def weights_body(pieces, bias, gu_ref, gd_ref, gb_ref, down):
    for j in range(16):
        for k, ref in enumerate((gu_ref, down)):
            for q in range(2):
                first = k * 32 + q * 16
                pair = pieces[j, first : first + 16, :].astype(F32)
                for h in range(2):
                    g = 2 * q + h
                    ref[j * 8 : (j + 1) * 8, g * 128 : (g + 1) * 128] = pair[h * 8 : (h + 1) * 8]
    gd_ref[...] = down[...].T
    gb_ref[...] = bias[0:4, :]


def flip(value, axis, size, mask):
    return lax.ppermute(value, axis, [(i, i ^ mask) for i in range(size)])


def in_order(axis, mine, theirs):
    low = lax.axis_index(axis) == 0
    return jnp.where(low, mine, theirs), jnp.where(low, theirs, mine)


def per_device(inputs, cotangent, basis, mode_weights, w_up, b_up, w_down):
    x_at = lax.axis_index("x").reshape(1)
    vertices = inputs.shape[1]

    *chunks, own = project(x_at, basis, inputs, cotangent)
    inputs, cotangent, chunks = lax.optimization_barrier((inputs, cotangent, chunks))
    arrived = [
        lax.ppermute(chunks[s - 1], "x", [(i, (i + s) % RING) for i in range(RING)])
        for s in (2, 1, 3)
    ]
    point, gu, gd, gb = pointwise(
        inputs.reshape(-1, 128), cotangent.reshape(-1, 128), w_up, b_up.reshape(1, 512), w_down
    )
    packed = small(
        pack_body, "pack", jax.ShapeDtypeStruct((16, 144, 128), BF16), own, *arrived, gu, gd, gb
    )
    messages = lax.all_to_all(packed, ("zlo", "y"), 0, 0)
    sums, coef = small(
        own_body,
        "own",
        [jax.ShapeDtypeStruct((144, 128), F32), jax.ShapeDtypeStruct((64, OWNED, 256), BF16)],
        messages,
        mode_weights,
    )
    coef = lax.all_to_all(coef, VERT, 0, 0).reshape(1024, 256)
    grad_input = finish(basis, coef, point.reshape(2, vertices, 128))

    other = flip(sums, "core", 2, 1)
    held = jnp.concatenate(in_order("core", sums[:64], other[:64]), axis=0)
    grads = sums[64:] + other[64:]
    other = flip(jnp.concatenate([held, grads], axis=0), "zhi", 2, 1)
    everyone = jnp.concatenate(in_order("zhi", held, other[:128]), axis=0)
    grads = grads + other[128:]
    grads = grads + flip(grads, "x", RING, 1)
    grads = grads + flip(grads, "x", RING, 3)
    pieces = jnp.broadcast_to(grads[:64].astype(BF16)[None], (16, 64, 128))
    pieces = lax.all_to_all(pieces, ("zlo", "y"), 0, 0)
    grad_w_up, grad_w_down, grad_b_up = pl.pallas_call(
        weights_body,
        out_shape=[
            jax.ShapeDtypeStruct((128, 512), F32),
            jax.ShapeDtypeStruct((512, 128), F32),
            jax.ShapeDtypeStruct((4, 128), F32),
        ],
        scratch_shapes=[pltpu.VMEM((128, 512), F32)],
        name="weights",
    )(pieces, grads[64:])

    everyone = everyone.reshape(RING, 2, 2, OWNED, 128)
    grad_modes = jnp.einsum(
        "gskc,gskd->kcd", everyone[:, :, 0], everyone[:, :, 1], precision=lax.Precision.HIGHEST
    )
    return (grad_input, grad_modes, grad_w_up, grad_b_up.reshape(512), grad_w_down)


def solution(mesh):
    fine = Mesh(mesh.devices.reshape(2, 2, RING, RING, RING), SAMP + VERT)
    in_specs = (
        P(SAMP, VERT, None),
        P(SAMP, VERT, None),
        P(VERT, None),
        P(VERT, None, None),
        P(),
        P(),
        P(),
    )
    out_specs = (P(SAMP, VERT, None), P(VERT, None, None), P(), P(), P())
    return jax.shard_map(
        per_device, mesh=fine, in_specs=in_specs, out_specs=out_specs, check_vma=False
    )
```

```python
import functools

import jax
import jax.numpy as jnp
from jax import lax
from jax.experimental import pallas as pl
from jax.experimental.pallas import tpu as pltpu
from jax.sharding import Mesh
from jax.sharding import PartitionSpec as P

F32 = jnp.float32
BF16 = jnp.bfloat16
ROOT = 0.7978845608
CUBE = 0.044715
RING = 4
OWNED = 16
SAMP = ("zhi", "core")
VERT = ("x", "zlo", "y")
MIB = 1 << 20


def product(a, b, a_dim, b_dim):
    return lax.dot_general(a, b, (((a_dim,), (b_dim,)), ((), ())), preferred_element_type=F32)


def whole(shape):
    return pl.BlockSpec(shape, lambda *_: (0,) * len(shape))


def project_body(basis_ref, inputs_ref, cotangent_ref, out, total):
    step = pl.program_id(0)

    @pl.when(step == 0)
    def _():
        total[...] = jnp.zeros_like(total)

    fields = jnp.concatenate(
        [inputs_ref[0], cotangent_ref[0], inputs_ref[1], cotangent_ref[1]], axis=1
    )
    total[...] += product(basis_ref[...], fields, 0, 0)

    @pl.when(step == pl.num_programs(0) - 1)
    def _():
        for x in range(RING):
            for y in range(RING):
                for z in range(RING):
                    first = x * 256 + z * 64 + y * 16
                    out[x * RING + y, z * 16 : (z + 1) * 16, :] = total[
                        first : first + 16, :
                    ].astype(BF16)


def project(basis, inputs, cotangent, rows=1024):
    field = pl.BlockSpec((2, rows, 128), lambda i: (0, i, 0))
    return pl.pallas_call(
        project_body,
        grid=(basis.shape[0] // rows,),
        in_specs=[pl.BlockSpec((rows, 1024), lambda i: (i, 0)), field, field],
        out_specs=whole((16, 64, 512)),
        scratch_shapes=[pltpu.VMEM((1024, 512), F32)],
        out_shape=jax.ShapeDtypeStruct((16, 64, 512), BF16),
        compiler_params=pltpu.CompilerParams(vmem_limit_bytes=56 * MIB),
        cost_estimate=pl.CostEstimate(
            flops=2 * 4096 * 1024 * 512, bytes_accessed=13 * MIB, transcendentals=0
        ),
        name="project",
    )(basis, inputs, cotangent)


def pointwise_body(x_ref, c_ref, up_ref, bias_ref, down_ref, p_ref, gu_ref, gd_ref, gb_ref):
    @pl.when(pl.program_id(0) == 0)
    def _():
        gu_ref[...] = jnp.zeros_like(gu_ref)
        gd_ref[...] = jnp.zeros_like(gd_ref)
        gb_ref[...] = jnp.zeros_like(gb_ref)

    up, down = up_ref[...], down_ref[...]
    x, c = x_ref[...], c_ref[...]
    z = product(x, up, 1, 0) + bias_ref[...]
    square = z * z
    t = jnp.tanh(z * (ROOT + (ROOT * CUBE) * square))
    half = 0.5 * z
    plus = 1.0 + t
    hidden = (half * plus).astype(BF16)
    slope = 0.5 * plus + half * (1.0 - t * t) * (ROOT + (3.0 * CUBE * ROOT) * square)
    grad_pre = (product(c, down, 1, 1) * slope).astype(BF16)
    p_ref[...] = product(grad_pre, up, 1, 1)
    with_ones = jnp.concatenate([x, jnp.ones((x.shape[0], 128), BF16)], axis=1)
    sums = product(with_ones, grad_pre, 0, 0)
    gu_ref[...] += sums[:128]
    gb_ref[...] += sums[128:136]
    gd_ref[...] += product(c, hidden, 0, 0)


def pointwise(x, c, up, bias, down, rows=1024):
    count = x.shape[0] // rows
    moving = pl.BlockSpec((rows, 128), lambda i: (i, 0))
    sums = [(128, 512), (128, 512), (8, 512)]
    return pl.pallas_call(
        pointwise_body,
        grid=(count,),
        in_specs=[moving, moving, whole((128, 512)), whole((1, 512)), whole((512, 128))],
        out_specs=[moving] + [whole(s) for s in sums],
        out_shape=[jax.ShapeDtypeStruct(s, F32) for s in [x.shape] + sums],
        compiler_params=pltpu.CompilerParams(vmem_limit_bytes=52 * MIB),
        cost_estimate=pl.CostEstimate(
            flops=10 * count * rows * 128 * 512,
            bytes_accessed=count * rows * 128 * 8,
            transcendentals=count * rows * 512,
        ),
        name="pointwise",
    )(x, c, up, bias, down)


def pack_body(gu, gd, gb, out):
    row = lax.broadcasted_iota(jnp.int32, (8, 128), 0)
    bias = jnp.zeros((8, 128), F32)
    for g in range(4):
        bias = jnp.where(row == g, gb[:, g * 128 : (g + 1) * 128], bias)
    for j in range(16):
        tiles = [
            ref[j * 8 : (j + 1) * 8, g * 128 : (g + 1) * 128] for ref in (gu, gd) for g in range(4)
        ]
        out[j] = jnp.concatenate(tiles + [bias], axis=0).astype(BF16)


def small(body, name, out_shape, *args, scratch=()):
    return pl.pallas_call(
        body,
        out_shape=out_shape,
        in_specs=[
            pl.BlockSpec(memory_space=pltpu.SMEM if v.dtype == jnp.int32 else pltpu.VMEM)
            for v in args
        ],
        scratch_shapes=list(scratch),
        compiler_params=pltpu.CompilerParams(vmem_limit_bytes=32 * MIB),
        name=name,
    )(*args)


def line_body(z_at, messages, own, one, two, three, total):
    sums = messages[0].astype(F32)
    for j in range(1, 16):
        sums = sums + messages[j].astype(F32)
    total[...] = sums
    for shift, out in enumerate((own, one, two, three)):
        first = pl.multiple_of(lax.rem(z_at[0] + shift, RING) * 16, 16)
        out[...] = total[pl.ds(first, 16), :]


def own_body(own, one, two, three, weights, pieces, modes_ref, line_ref):
    total = (own[...] + two[...]) + (one[...] + three[...])
    for g in range(4):
        modes_ref[g * 16 : (g + 1) * 16, :] = total[:, g * 128 : (g + 1) * 128].astype(BF16)
    grads = pieces[0].astype(F32)
    for j in range(1, 16):
        grads = grads + pieces[j].astype(F32)
    parts = []
    for sample in range(2):
        rest = total[:, sample * 256 + 128 : sample * 256 + 256]
        for _ in range(3):
            parts.append(rest.astype(BF16))
            rest = rest - parts[-1].astype(F32)
    left = jnp.concatenate(parts, axis=0)
    row = lax.broadcasted_iota(jnp.int32, (16, 128), 0)
    first = jnp.zeros((16, 128), F32)
    second = jnp.zeros((16, 128), F32)
    for k in range(16):
        mixed = product(left, weights[k], 1, 1)
        first = jnp.where(row == k, mixed[0:16] + mixed[16:32] + mixed[32:48], first)
        second = jnp.where(row == k, mixed[48:64] + mixed[64:80] + mixed[80:96], second)
    line_ref[...] = jnp.concatenate([first, second, grads], axis=0).astype(BF16)


def gather_body(z_at, own, one, two, three, modes, coef_ref, samp_ref, held):
    for shift, ref in enumerate((own, one, two, three)):
        held[lax.rem(z_at[0] + RING - shift, RING)] = ref[0:32, :]
    coef = held[...].reshape(128, 128)
    for v in range(16):
        coef_ref[v] = coef
    parts = [ref[32:104, :].astype(F32) for ref in (own, one, two, three)]
    grads = (parts[0] + parts[2]) + (parts[1] + parts[3])
    samp_ref[0:64, :] = modes[...]
    samp_ref[64:136, :] = grads.astype(BF16)


def join_body(at, own, core, zhi, both, everyone, bias, message):
    for mask, ref in enumerate((own, core, zhi, both)):
        everyone[jnp.bitwise_xor(at[0], mask)] = ref[0:64, :]
    parts = [ref[64:136, :].astype(F32) for ref in (own, core, zhi, both)]
    grads = (parts[0] + parts[1]) + (parts[2] + parts[3])
    bias[...] = grads[64:72]
    body = grads[0:64].astype(BF16)
    for v in range(16):
        message[v] = body


def finish_body(basis_ref, message_ref, p_ref, out_ref, coef):
    @pl.when(pl.program_id(0) == 0)
    def _():
        for x in range(RING):
            for y in range(RING):
                for z in range(RING):
                    first = x * 256 + z * 64 + y * 16
                    for half in range(2):
                        coef[first : first + 16, half * 128 : (half + 1) * 128] = message_ref[
                            x * RING + y, z * 32 + half * 16 : z * 32 + half * 16 + 16, :
                        ]

    total = product(basis_ref[...], coef[...], 1, 0)
    out_ref[0] = (total[:, :128] + p_ref[0]).astype(out_ref.dtype)
    out_ref[1] = (total[:, 128:] + p_ref[1]).astype(out_ref.dtype)


def finish(basis, message, point, rows=1024):
    vertices = basis.shape[0]
    both = pl.BlockSpec((2, rows, 128), lambda i: (0, i, 0))
    return pl.pallas_call(
        finish_body,
        grid=(vertices // rows,),
        in_specs=[pl.BlockSpec((rows, 1024), lambda i: (i, 0)), whole(message.shape), both],
        out_specs=both,
        out_shape=jax.ShapeDtypeStruct((2, vertices, 128), BF16),
        scratch_shapes=[pltpu.VMEM((1024, 256), BF16)],
        compiler_params=pltpu.CompilerParams(vmem_limit_bytes=56 * MIB),
        cost_estimate=pl.CostEstimate(
            flops=2 * vertices * 1024 * 256, bytes_accessed=16 * MIB, transcendentals=0
        ),
        name="finish",
    )(basis, message, point)


def weights_body(message, gu_ref, gd_ref, down):
    for j in range(16):
        tiles = message[j].astype(F32)
        for k, ref in enumerate((gu_ref, down)):
            for g in range(4):
                first = k * 32 + g * 8
                ref[j * 8 : (j + 1) * 8, g * 128 : (g + 1) * 128] = tiles[first : first + 8]
    gd_ref[...] = down[...].T


def shift(value, axis, by):
    return lax.ppermute(value, axis, [(i, (i + by) % RING) for i in range(RING)])


def per_device(inputs, cotangent, basis, mode_weights, w_up, b_up, w_down):
    z_at = lax.axis_index("zlo").reshape(1)
    samp_at = (lax.axis_index("zhi") * 2 + lax.axis_index("core")).reshape(1)
    vertices = inputs.shape[1]
    struct = jax.ShapeDtypeStruct

    packed = project(basis, inputs, cotangent)
    inputs, cotangent, packed = lax.optimization_barrier((inputs, cotangent, packed))
    messages = lax.all_to_all(packed, ("x", "y"), 0, 0)
    point, gu, gd, gb = pointwise(
        inputs.reshape(-1, 128), cotangent.reshape(-1, 128), w_up, b_up.reshape(1, 512), w_down
    )
    torus = ("x", "y")
    pieces = lax.all_to_all(
        small(pack_body, "pack", struct((16, 72, 128), BF16), gu, gd, gb), torus, 0, 0
    )
    own, *chunks = small(
        line_body, "line", [struct((16, 512), F32)] * 4,
        z_at, messages, scratch=[pltpu.VMEM((64, 512), F32)],
    )
    arrived = [shift(chunks[s - 1], "zlo", s) for s in (1, 2, 3)]
    modes, line = small(
        own_body, "own", [struct((64, 128), BF16), struct((104, 128), BF16)],
        own, *arrived, mode_weights, pieces,
    )
    coef, samp = small(
        gather_body, "gather", [struct((16, 128, 128), BF16), struct((136, 128), BF16)],
        z_at, line, *[shift(line, "zlo", s) for s in (1, 2, 3)], modes,
        scratch=[pltpu.VMEM((RING, 32, 128), BF16)],
    )
    coef = lax.all_to_all(coef, torus, 0, 0)
    core = lax.ppermute(samp, "core", [(0, 1), (1, 0)])
    zhi = lax.ppermute(samp, "zhi", [(0, 1), (1, 0)])
    both = lax.ppermute(samp, SAMP, [(i, 3 - i) for i in range(RING)])
    everyone, bias, message = small(
        join_body, "join",
        [struct((RING, 64, 128), BF16), struct((8, 128), F32), struct((16, 64, 128), BF16)],
        samp_at, samp, core, zhi, both,
    )
    coef, message = lax.optimization_barrier((coef, message))
    message = lax.all_to_all(message, torus, 0, 0)
    grad_input = finish(basis, coef, point.reshape(2, vertices, 128))
    grad_w_up, grad_w_down = small(
        weights_body, "weights", [struct((128, 512), F32), struct((512, 128), F32)],
        message, scratch=[pltpu.VMEM((128, 512), F32)],
    )
    everyone = everyone.reshape(RING, 2, 2, OWNED, 128)
    grad_modes = jnp.einsum(
        "gskc,gskd->kcd", everyone[:, :, 0], everyone[:, :, 1], preferred_element_type=F32
    )
    return (grad_input, grad_modes, grad_w_up, bias[:4].reshape(512), grad_w_down)


def solution(mesh):
    fine = Mesh(mesh.devices.reshape(2, 2, RING, RING, RING), SAMP + VERT)
    in_specs = (
        P(SAMP, VERT, None),
        P(SAMP, VERT, None),
        P(VERT, None),
        P(VERT, None, None),
        P(),
        P(),
        P(),
    )
    out_specs = (P(SAMP, VERT, None), P(VERT, None, None), P(), P(), P())
    return jax.shard_map(
        per_device, mesh=fine, in_specs=in_specs, out_specs=out_specs, check_vma=False
    )
```

```python
import functools

import jax
import jax.numpy as jnp
from jax import lax
from jax.experimental import pallas as pl
from jax.experimental.pallas import tpu as pltpu
from jax.sharding import Mesh
from jax.sharding import PartitionSpec as P

F32 = jnp.float32
BF16 = jnp.bfloat16
ROOT = 0.7978845608
CUBE = 0.044715
RING = 4
OWNED = 16
SAMP = ("zhi", "core")
VERT = ("x", "zlo", "y")
MIB = 1 << 20


def product(a, b, a_dim, b_dim):
    return lax.dot_general(a, b, (((a_dim,), (b_dim,)), ((), ())), preferred_element_type=F32)


PIECES = 8
AHEAD = 3
VMEM = pl.BlockSpec(memory_space=pltpu.VMEM)
HBM = pl.BlockSpec(memory_space=pltpu.HBM)


def project_body(basis_hbm, x_hbm, c_hbm, out, basis, x, c, total, sems):
    rows = basis.shape[0] // PIECES

    def copies(i):
        at = pl.ds(i * rows, rows)
        return [
            pltpu.make_async_copy(basis_hbm.at[at], basis.at[at], sems.at[0, i]),
            pltpu.make_async_copy(x_hbm.at[:, at], x.at[:, at], sems.at[1, i]),
            pltpu.make_async_copy(c_hbm.at[:, at], c.at[:, at], sems.at[2, i]),
        ]

    for i in range(AHEAD):
        for copy in copies(i):
            copy.start()
    for i in range(PIECES):
        for copy in copies(i):
            copy.wait()
        if i + AHEAD < PIECES:
            for copy in copies(i + AHEAD):
                copy.start()
        at = slice(i * rows, (i + 1) * rows)
        fields = jnp.concatenate([x[0, at], c[0, at], x[1, at], c[1, at]], axis=1)
        part = product(basis[at], fields, 0, 0)
        if i == 0:
            total[...] = part
        else:
            total[...] += part
    for x_at in range(RING):
        for y in range(RING):
            for z in range(RING):
                first = x_at * 256 + z * 64 + y * 16
                out[x_at * RING + y, z * 16 : (z + 1) * 16, :] = total[
                    first : first + 16, :
                ].astype(BF16)


def project(basis, inputs, cotangent):
    return pl.pallas_call(
        project_body,
        in_specs=[HBM] * 3,
        out_specs=VMEM,
        out_shape=jax.ShapeDtypeStruct((16, 64, 512), BF16),
        scratch_shapes=[
            pltpu.VMEM(basis.shape, BF16),
            pltpu.VMEM(inputs.shape, BF16),
            pltpu.VMEM(cotangent.shape, BF16),
            pltpu.VMEM((1024, 512), F32),
            pltpu.SemaphoreType.DMA((3, PIECES)),
        ],
        compiler_params=pltpu.CompilerParams(vmem_limit_bytes=56 * MIB),
        cost_estimate=pl.CostEstimate(
            flops=2 * 4096 * 1024 * 512, bytes_accessed=13 * MIB, transcendentals=0
        ),
        name="project",
    )(basis, inputs, cotangent)


def pointwise_body(
    x_hbm, c_hbm, up_ref, bias_ref, down_ref, p_hbm, gu_ref, gd_ref, gb_ref, x_ref, c_ref, p_ref, sems
):
    rows = 2048
    count = x_ref.shape[0] // rows

    def copy(k, i, at):
        if k == 2:
            return pltpu.make_async_copy(p_ref.at[at], p_hbm.at[at], sems.at[2, i])
        source, held = ((x_hbm, x_ref), (c_hbm, c_ref))[k]
        return pltpu.make_async_copy(source.at[at], held.at[at], sems.at[k, i])

    def load(i):
        at = pl.ds(pl.multiple_of(i * rows, rows), rows)
        copy(0, i, at).start()
        copy(1, i, at).start()

    load(0)
    gu_ref[...] = jnp.zeros_like(gu_ref)
    gd_ref[...] = jnp.zeros_like(gd_ref)
    gb_ref[...] = jnp.zeros_like(gb_ref)

    @pl.loop(0, count)
    def _(i):
        at = pl.ds(pl.multiple_of(i * rows, rows), rows)
        copy(0, i, at).wait()
        copy(1, i, at).wait()

        @pl.when(i + 1 < count)
        def _():
            load(i + 1)

        up, down = up_ref[...], down_ref[...]
        x, c = x_ref[at, :], c_ref[at, :]
        z = product(x, up, 1, 0) + bias_ref[...]
        square = z * z
        q = 0.5 + 0.5 * jnp.tanh(z * (ROOT + (ROOT * CUBE) * square))
        value = z * q
        hidden = value.astype(BF16)
        slope = q + (value - value * q) * (2.0 * ROOT + (6.0 * CUBE * ROOT) * square)
        grad_pre = (product(c, down, 1, 1) * slope).astype(BF16)
        p_ref[at, :] = product(grad_pre, up, 1, 1).astype(BF16)
        copy(2, i, at).start()
        with_ones = jnp.concatenate([x, jnp.ones((rows, 128), BF16)], axis=1)
        sums = product(with_ones, grad_pre, 0, 0)
        gu_ref[...] += sums[:128]
        gb_ref[...] += sums[128:136]
        gd_ref[...] += product(c, hidden, 0, 0)

    for i in range(count):
        copy(2, i, pl.ds(i * rows, rows)).wait()


def pointwise(x, c, up, bias, down):
    rows = x.shape[0]
    return pl.pallas_call(
        pointwise_body,
        in_specs=[HBM, HBM] + [VMEM] * 3,
        out_specs=[HBM] + [VMEM] * 3,
        out_shape=[jax.ShapeDtypeStruct(x.shape, BF16)]
        + [jax.ShapeDtypeStruct(s, F32) for s in ((128, 512), (128, 512), (8, 512))],
        scratch_shapes=[
            pltpu.VMEM(x.shape, BF16),
            pltpu.VMEM(c.shape, BF16),
            pltpu.VMEM(x.shape, BF16),
            pltpu.SemaphoreType.DMA((3, 4)),
        ],
        compiler_params=pltpu.CompilerParams(vmem_limit_bytes=52 * MIB),
        cost_estimate=pl.CostEstimate(
            flops=10 * rows * 128 * 512, bytes_accessed=rows * 128 * 8, transcendentals=rows * 512
        ),
        name="pointwise",
    )(x, c, up, bias, down)


def pack_body(gu, gd, gb, out):
    row = lax.broadcasted_iota(jnp.int32, (8, 128), 0)
    bias = jnp.zeros((8, 128), F32)
    for g in range(4):
        bias = jnp.where(row == g, gb[:, g * 128 : (g + 1) * 128], bias)
    for j in range(16):
        tiles = [
            ref[j * 8 : (j + 1) * 8, g * 128 : (g + 1) * 128] for ref in (gu, gd) for g in range(4)
        ]
        out[j] = jnp.concatenate(tiles + [bias], axis=0).astype(BF16)


def small(body, name, out_shape, *args, scratch=()):
    return pl.pallas_call(
        body,
        out_shape=out_shape,
        in_specs=[
            pl.BlockSpec(memory_space=pltpu.SMEM if v.dtype == jnp.int32 else pltpu.VMEM)
            for v in args
        ],
        scratch_shapes=list(scratch),
        compiler_params=pltpu.CompilerParams(vmem_limit_bytes=32 * MIB),
        name=name,
    )(*args)


def line_body(z_at, messages, own, one, two, three, total):
    sums = messages[0].astype(F32)
    for j in range(1, 16):
        sums = sums + messages[j].astype(F32)
    total[...] = sums
    for shift, out in enumerate((own, one, two, three)):
        first = pl.multiple_of(lax.rem(z_at[0] + shift, RING) * 16, 16)
        out[...] = total[pl.ds(first, 16), :]


def own_body(own, one, two, three, weights, pieces, modes_ref, line_ref):
    total = (own[...] + two[...]) + (one[...] + three[...])
    for g in range(4):
        modes_ref[g * 16 : (g + 1) * 16, :] = total[:, g * 128 : (g + 1) * 128].astype(BF16)
    grads = pieces[0].astype(F32)
    for j in range(1, 16):
        grads = grads + pieces[j].astype(F32)
    parts = []
    for sample in range(2):
        rest = total[:, sample * 256 + 128 : sample * 256 + 256]
        for _ in range(3):
            parts.append(rest.astype(BF16))
            rest = rest - parts[-1].astype(F32)
    left = jnp.concatenate(parts, axis=0)
    row = lax.broadcasted_iota(jnp.int32, (16, 128), 0)
    first = jnp.zeros((16, 128), F32)
    second = jnp.zeros((16, 128), F32)
    for k in range(16):
        mixed = product(left, weights[k], 1, 1)
        first = jnp.where(row == k, mixed[0:16] + mixed[16:32] + mixed[32:48], first)
        second = jnp.where(row == k, mixed[48:64] + mixed[64:80] + mixed[80:96], second)
    line_ref[...] = jnp.concatenate([first, second, grads], axis=0).astype(BF16)


def gather_body(z_at, own, one, two, three, modes, coef_ref, samp_ref, held):
    for shift, ref in enumerate((own, one, two, three)):
        held[lax.rem(z_at[0] + RING - shift, RING)] = ref[0:32, :]
    coef = held[...].reshape(128, 128)
    for v in range(16):
        coef_ref[v] = coef
    parts = [ref[32:104, :].astype(F32) for ref in (own, one, two, three)]
    grads = (parts[0] + parts[2]) + (parts[1] + parts[3])
    samp_ref[0:64, :] = modes[...]
    samp_ref[64:136, :] = grads.astype(BF16)


def join_body(at, own, core, zhi, both, everyone, bias, message):
    for mask, ref in enumerate((own, core, zhi, both)):
        everyone[jnp.bitwise_xor(at[0], mask)] = ref[0:64, :]
    parts = [ref[64:136, :].astype(F32) for ref in (own, core, zhi, both)]
    grads = (parts[0] + parts[1]) + (parts[2] + parts[3])
    bias[...] = grads[64:72]
    body = grads[0:64].astype(BF16)
    for v in range(16):
        message[v] = body


def finish_body(basis_ref, message_ref, p_ref, out_ref, coef):
    @pl.when(pl.program_id(0) == 0)
    def _():
        for x in range(RING):
            for y in range(RING):
                for z in range(RING):
                    first = x * 256 + z * 64 + y * 16
                    for half in range(2):
                        coef[first : first + 16, half * 128 : (half + 1) * 128] = message_ref[
                            x * RING + y, z * 32 + half * 16 : z * 32 + half * 16 + 16, :
                        ]

    total = product(basis_ref[...], coef[...], 1, 0)
    out_ref[0] = (total[:, :128] + p_ref[0].astype(F32)).astype(out_ref.dtype)
    out_ref[1] = (total[:, 128:] + p_ref[1].astype(F32)).astype(out_ref.dtype)


def finish(basis, message, point, rows=2048):
    vertices = basis.shape[0]
    both = pl.BlockSpec((2, rows, 128), lambda i: (0, i, 0))
    return pl.pallas_call(
        finish_body,
        grid=(vertices // rows,),
        in_specs=[
            pl.BlockSpec((rows, 1024), lambda i: (i, 0)),
            pl.BlockSpec(message.shape, lambda i: (0, 0, 0)),
            both,
        ],
        out_specs=both,
        out_shape=jax.ShapeDtypeStruct((2, vertices, 128), BF16),
        scratch_shapes=[pltpu.VMEM((1024, 256), BF16)],
        compiler_params=pltpu.CompilerParams(vmem_limit_bytes=56 * MIB),
        cost_estimate=pl.CostEstimate(
            flops=2 * vertices * 1024 * 256, bytes_accessed=16 * MIB, transcendentals=0
        ),
        name="finish",
    )(basis, message, point)


def weights_body(message, gu_ref, gd_ref, down):
    for j in range(16):
        tiles = message[j].astype(F32)
        for k, ref in enumerate((gu_ref, down)):
            for g in range(4):
                first = k * 32 + g * 8
                ref[j * 8 : (j + 1) * 8, g * 128 : (g + 1) * 128] = tiles[first : first + 8]
    gd_ref[...] = down[...].T


def shift(value, axis, by):
    return lax.ppermute(value, axis, [(i, (i + by) % RING) for i in range(RING)])


def per_device(inputs, cotangent, basis, mode_weights, w_up, b_up, w_down):
    z_at = lax.axis_index("zlo").reshape(1)
    samp_at = (lax.axis_index("zhi") * 2 + lax.axis_index("core")).reshape(1)
    vertices = inputs.shape[1]
    struct = jax.ShapeDtypeStruct

    packed = project(basis, inputs, cotangent)
    inputs, cotangent, packed = lax.optimization_barrier((inputs, cotangent, packed))
    messages = lax.all_to_all(packed, ("x", "y"), 0, 0)
    point, gu, gd, gb = pointwise(
        inputs.reshape(-1, 128), cotangent.reshape(-1, 128), w_up, b_up.reshape(1, 512), w_down
    )
    torus = ("x", "y")
    pieces = lax.all_to_all(
        small(pack_body, "pack", struct((16, 72, 128), BF16), gu, gd, gb), torus, 0, 0
    )
    own, *chunks = small(
        line_body, "line", [struct((16, 512), F32)] * 4,
        z_at, messages, scratch=[pltpu.VMEM((64, 512), F32)],
    )
    arrived = [shift(chunks[s - 1], "zlo", s) for s in (1, 2, 3)]
    modes, line = small(
        own_body, "own", [struct((64, 128), BF16), struct((104, 128), BF16)],
        own, *arrived, mode_weights, pieces,
    )
    coef, samp = small(
        gather_body, "gather", [struct((16, 128, 128), BF16), struct((136, 128), BF16)],
        z_at, line, *[shift(line, "zlo", s) for s in (1, 2, 3)], modes,
        scratch=[pltpu.VMEM((RING, 32, 128), BF16)],
    )
    coef = lax.all_to_all(coef, torus, 0, 0)
    core = lax.ppermute(samp, "core", [(0, 1), (1, 0)])
    zhi = lax.ppermute(samp, "zhi", [(0, 1), (1, 0)])
    both = lax.ppermute(samp, SAMP, [(i, 3 - i) for i in range(RING)])
    everyone, bias, message = small(
        join_body, "join",
        [struct((RING, 64, 128), BF16), struct((8, 128), F32), struct((16, 64, 128), BF16)],
        samp_at, samp, core, zhi, both,
    )
    coef, message = lax.optimization_barrier((coef, message))
    message = lax.all_to_all(message, torus, 0, 0)
    grad_input = finish(basis, coef, point.reshape(2, vertices, 128))
    grad_w_up, grad_w_down = small(
        weights_body, "weights", [struct((128, 512), F32), struct((512, 128), F32)],
        message, scratch=[pltpu.VMEM((128, 512), F32)],
    )
    everyone = everyone.reshape(RING, 2, 2, OWNED, 128)
    grad_modes = jnp.einsum(
        "gskc,gskd->kcd", everyone[:, :, 0], everyone[:, :, 1], preferred_element_type=F32
    )
    return (grad_input, grad_modes, grad_w_up, bias[:4].reshape(512), grad_w_down)


def solution(mesh):
    fine = Mesh(mesh.devices.reshape(2, 2, RING, RING, RING), SAMP + VERT)
    in_specs = (
        P(SAMP, VERT, None),
        P(SAMP, VERT, None),
        P(VERT, None),
        P(VERT, None, None),
        P(),
        P(),
        P(),
    )
    out_specs = (P(SAMP, VERT, None), P(VERT, None, None), P(), P(), P())
    return jax.shard_map(
        per_device, mesh=fine, in_specs=in_specs, out_specs=out_specs, check_vma=False
    )
```

```python
import functools

import jax
import jax.numpy as jnp
from jax import lax
from jax.experimental import pallas as pl
from jax.experimental.pallas import tpu as pltpu
from jax.sharding import Mesh
from jax.sharding import PartitionSpec as P

F32 = jnp.float32
BF16 = jnp.bfloat16
ROOT = 0.7978845608
CUBE = 0.044715
RING = 4
OWNED = 16
SAMP = ("zhi", "core")
VERT = ("x", "zlo", "y")
MIB = 1 << 20


def product(a, b, a_dim, b_dim):
    return lax.dot_general(a, b, (((a_dim,), (b_dim,)), ((), ())), preferred_element_type=F32)


PIECES = 8
AHEAD = 3
VMEM = pl.BlockSpec(memory_space=pltpu.VMEM)
HBM = pl.BlockSpec(memory_space=pltpu.HBM)


def project_body(basis_hbm, x_hbm, c_hbm, out, basis, x, c, total, sems):
    rows = basis.shape[0] // PIECES

    def copies(i):
        at = pl.ds(i * rows, rows)
        return [
            pltpu.make_async_copy(basis_hbm.at[at], basis.at[at], sems.at[0, i]),
            pltpu.make_async_copy(x_hbm.at[:, at], x.at[:, at], sems.at[1, i]),
            pltpu.make_async_copy(c_hbm.at[:, at], c.at[:, at], sems.at[2, i]),
        ]

    for i in range(AHEAD):
        for copy in copies(i):
            copy.start()
    for i in range(PIECES):
        for copy in copies(i):
            copy.wait()
        if i + AHEAD < PIECES:
            for copy in copies(i + AHEAD):
                copy.start()
        at = slice(i * rows, (i + 1) * rows)
        fields = jnp.concatenate([x[0, at], c[0, at], x[1, at], c[1, at]], axis=1)
        part = product(basis[at], fields, 0, 0)
        if i == 0:
            total[...] = part
        else:
            total[...] += part
    for x_at in range(RING):
        for y in range(RING):
            for z in range(RING):
                first = x_at * 256 + z * 64 + y * 16
                out[x_at * RING + y, z * 16 : (z + 1) * 16, :] = total[
                    first : first + 16, :
                ].astype(BF16)


def project(basis, inputs, cotangent):
    return pl.pallas_call(
        project_body,
        in_specs=[HBM] * 3,
        out_specs=VMEM,
        out_shape=jax.ShapeDtypeStruct((16, 64, 512), BF16),
        scratch_shapes=[
            pltpu.VMEM(basis.shape, BF16),
            pltpu.VMEM(inputs.shape, BF16),
            pltpu.VMEM(cotangent.shape, BF16),
            pltpu.VMEM((1024, 512), F32),
            pltpu.SemaphoreType.DMA((3, PIECES)),
        ],
        compiler_params=pltpu.CompilerParams(vmem_limit_bytes=56 * MIB),
        cost_estimate=pl.CostEstimate(
            flops=2 * 4096 * 1024 * 512, bytes_accessed=13 * MIB, transcendentals=0
        ),
        name="project",
    )(basis, inputs, cotangent)


def pointwise_body(
    x_hbm, c_hbm, up_ref, bias_ref, down_ref, p_hbm, gu_ref, gd_ref, gb_ref, x_ref, c_ref, p_ref, sems
):
    rows = 2048
    count = x_ref.shape[0] // rows

    def copy(k, i, at):
        if k == 2:
            return pltpu.make_async_copy(p_ref.at[at], p_hbm.at[at], sems.at[2, i])
        source, held = ((x_hbm, x_ref), (c_hbm, c_ref))[k]
        return pltpu.make_async_copy(source.at[at], held.at[at], sems.at[k, i])

    def load(i):
        at = pl.ds(pl.multiple_of(i * rows, rows), rows)
        copy(0, i, at).start()
        copy(1, i, at).start()

    load(0)
    gu_ref[...] = jnp.zeros_like(gu_ref)
    gd_ref[...] = jnp.zeros_like(gd_ref)
    gb_ref[...] = jnp.zeros_like(gb_ref)

    @pl.loop(0, count)
    def _(i):
        at = pl.ds(pl.multiple_of(i * rows, rows), rows)
        copy(0, i, at).wait()
        copy(1, i, at).wait()

        @pl.when(i + 1 < count)
        def _():
            load(i + 1)

        up, down = up_ref[...], down_ref[...]
        x, c = x_ref[at, :], c_ref[at, :]
        z = product(x, up, 1, 0) + bias_ref[...]
        square = z * z
        q = 0.5 + 0.5 * jnp.tanh(z * (ROOT + (ROOT * CUBE) * square))
        value = z * q
        hidden = value.astype(BF16)
        slope = q + (value - value * q) * (2.0 * ROOT + (6.0 * CUBE * ROOT) * square)
        exact = product(c, down, 1, 1) * slope
        gb_ref[...] += jnp.sum(exact.reshape(rows // 8, 8, 512), axis=0)
        grad_pre = exact.astype(BF16)
        p_ref[at, :] = product(grad_pre, up, 1, 1).astype(BF16)
        copy(2, i, at).start()
        gu_ref[...] += product(x, grad_pre, 0, 0)
        gd_ref[...] += product(c, hidden, 0, 0)

    for i in range(count):
        copy(2, i, pl.ds(i * rows, rows)).wait()


def pointwise(x, c, up, bias, down):
    rows = x.shape[0]
    return pl.pallas_call(
        pointwise_body,
        in_specs=[HBM, HBM] + [VMEM] * 3,
        out_specs=[HBM] + [VMEM] * 3,
        out_shape=[jax.ShapeDtypeStruct(x.shape, BF16)]
        + [jax.ShapeDtypeStruct(s, F32) for s in ((128, 512), (128, 512), (8, 512))],
        scratch_shapes=[
            pltpu.VMEM(x.shape, BF16),
            pltpu.VMEM(c.shape, BF16),
            pltpu.VMEM(x.shape, BF16),
            pltpu.SemaphoreType.DMA((3, 4)),
        ],
        compiler_params=pltpu.CompilerParams(vmem_limit_bytes=52 * MIB),
        cost_estimate=pl.CostEstimate(
            flops=10 * rows * 128 * 512, bytes_accessed=rows * 128 * 8, transcendentals=rows * 512
        ),
        name="pointwise",
    )(x, c, up, bias, down)


def pack_body(gu, gd, gb, out):
    row = lax.broadcasted_iota(jnp.int32, (8, 128), 0)
    sums = jnp.sum(gb[...], axis=0, keepdims=True)
    bias = jnp.zeros((8, 128), F32)
    for g in range(4):
        bias = jnp.where(row == g, sums[:, g * 128 : (g + 1) * 128], bias)
    for j in range(16):
        tiles = [
            ref[j * 8 : (j + 1) * 8, g * 128 : (g + 1) * 128] for ref in (gu, gd) for g in range(4)
        ]
        out[j] = jnp.concatenate(tiles + [bias], axis=0).astype(BF16)


def small(body, name, out_shape, *args, scratch=()):
    return pl.pallas_call(
        body,
        out_shape=out_shape,
        in_specs=[
            pl.BlockSpec(memory_space=pltpu.SMEM if v.dtype == jnp.int32 else pltpu.VMEM)
            for v in args
        ],
        scratch_shapes=list(scratch),
        compiler_params=pltpu.CompilerParams(vmem_limit_bytes=32 * MIB),
        name=name,
    )(*args)


def line_body(z_at, messages, own, one, two, three, total):
    sums = messages[0].astype(F32)
    for j in range(1, 16):
        sums = sums + messages[j].astype(F32)
    total[...] = sums
    for shift, out in enumerate((own, one, two, three)):
        first = pl.multiple_of(lax.rem(z_at[0] + shift, RING) * 16, 16)
        out[...] = total[pl.ds(first, 16), :]


def own_body(own, one, two, three, weights, pieces, modes_ref, line_ref):
    total = (own[...] + two[...]) + (one[...] + three[...])
    for g in range(4):
        modes_ref[g * 16 : (g + 1) * 16, :] = total[:, g * 128 : (g + 1) * 128].astype(BF16)
    grads = pieces[0].astype(F32)
    for j in range(1, 16):
        grads = grads + pieces[j].astype(F32)
    parts = []
    for sample in range(2):
        rest = total[:, sample * 256 + 128 : sample * 256 + 256]
        for _ in range(3):
            parts.append(rest.astype(BF16))
            rest = rest - parts[-1].astype(F32)
    left = jnp.concatenate(parts, axis=0)
    row = lax.broadcasted_iota(jnp.int32, (16, 128), 0)
    first = jnp.zeros((16, 128), F32)
    second = jnp.zeros((16, 128), F32)
    for k in range(16):
        mixed = product(left, weights[k], 1, 1)
        first = jnp.where(row == k, mixed[0:16] + mixed[16:32] + mixed[32:48], first)
        second = jnp.where(row == k, mixed[48:64] + mixed[64:80] + mixed[80:96], second)
    line_ref[...] = jnp.concatenate([first, second, grads], axis=0).astype(BF16)


def gather_body(z_at, own, one, two, three, modes, coef_ref, samp_ref, held):
    for shift, ref in enumerate((own, one, two, three)):
        held[lax.rem(z_at[0] + RING - shift, RING)] = ref[0:32, :]
    coef = held[...].reshape(128, 128)
    for v in range(16):
        coef_ref[v] = coef
    parts = [ref[32:104, :].astype(F32) for ref in (own, one, two, three)]
    grads = (parts[0] + parts[2]) + (parts[1] + parts[3])
    samp_ref[0:64, :] = modes[...]
    samp_ref[64:136, :] = grads.astype(BF16)


def join_body(at, own, both, zhi, core, everyone, bias, message):
    for mask, ref in enumerate((own, core, zhi, both)):
        everyone[jnp.bitwise_xor(at[0], mask)] = ref[0:64, :]
    parts = [ref[64:136, :].astype(F32) for ref in (own, core, zhi, both)]
    grads = (parts[0] + parts[1]) + (parts[2] + parts[3])
    bias[...] = grads[64:72]
    body = grads[0:64].astype(BF16)
    for v in range(16):
        message[v] = body


def finish_body(basis_ref, message_ref, p_ref, out_ref, coef):
    @pl.when(pl.program_id(0) == 0)
    def _():
        for x in range(RING):
            for y in range(RING):
                for z in range(RING):
                    first = x * 256 + z * 64 + y * 16
                    for half in range(2):
                        coef[first : first + 16, half * 128 : (half + 1) * 128] = message_ref[
                            x * RING + y, z * 32 + half * 16 : z * 32 + half * 16 + 16, :
                        ]

    total = product(basis_ref[...], coef[...], 1, 0)
    out_ref[0] = (total[:, :128] + p_ref[0].astype(F32)).astype(out_ref.dtype)
    out_ref[1] = (total[:, 128:] + p_ref[1].astype(F32)).astype(out_ref.dtype)


def finish(basis, message, point, rows=2048):
    vertices = basis.shape[0]
    both = pl.BlockSpec((2, rows, 128), lambda i: (0, i, 0))
    return pl.pallas_call(
        finish_body,
        grid=(vertices // rows,),
        in_specs=[
            pl.BlockSpec((rows, 1024), lambda i: (i, 0)),
            pl.BlockSpec(message.shape, lambda i: (0, 0, 0)),
            both,
        ],
        out_specs=both,
        out_shape=jax.ShapeDtypeStruct((2, vertices, 128), BF16),
        scratch_shapes=[pltpu.VMEM((1024, 256), BF16)],
        compiler_params=pltpu.CompilerParams(vmem_limit_bytes=56 * MIB),
        cost_estimate=pl.CostEstimate(
            flops=2 * vertices * 1024 * 256, bytes_accessed=16 * MIB, transcendentals=0
        ),
        name="finish",
    )(basis, message, point)


def weights_body(message, gu_ref, gd_ref, down):
    for j in range(16):
        tiles = message[j].astype(F32)
        for k, ref in enumerate((gu_ref, down)):
            for g in range(4):
                first = k * 32 + g * 8
                ref[j * 8 : (j + 1) * 8, g * 128 : (g + 1) * 128] = tiles[first : first + 8]
    gd_ref[...] = down[...].T


def shift(value, axis, by):
    return lax.ppermute(value, axis, [(i, (i + by) % RING) for i in range(RING)])


def per_device(inputs, cotangent, basis, mode_weights, w_up, b_up, w_down):
    z_at = lax.axis_index("zlo").reshape(1)
    samp_at = (lax.axis_index("zhi") * 2 + lax.axis_index("core")).reshape(1)
    vertices = inputs.shape[1]
    struct = jax.ShapeDtypeStruct

    packed = project(basis, inputs, cotangent)
    inputs, cotangent, packed = lax.optimization_barrier((inputs, cotangent, packed))
    messages = lax.all_to_all(packed, ("x", "y"), 0, 0)
    point, gu, gd, gb = pointwise(
        inputs.reshape(-1, 128), cotangent.reshape(-1, 128), w_up, b_up.reshape(1, 512), w_down
    )
    torus = ("x", "y")
    pieces = lax.all_to_all(
        small(pack_body, "pack", struct((16, 72, 128), BF16), gu, gd, gb), torus, 0, 0
    )
    own, *chunks = small(
        line_body, "line", [struct((16, 512), F32)] * 4,
        z_at, messages, scratch=[pltpu.VMEM((64, 512), F32)],
    )
    arrived = [shift(chunks[s - 1], "zlo", s) for s in (1, 2, 3)]
    modes, line = small(
        own_body, "own", [struct((64, 128), BF16), struct((104, 128), BF16)],
        own, *arrived, mode_weights, pieces,
    )
    coef, samp = small(
        gather_body, "gather", [struct((16, 128, 128), BF16), struct((136, 128), BF16)],
        z_at, line, *[shift(line, "zlo", s) for s in (1, 2, 3)], modes,
        scratch=[pltpu.VMEM((RING, 32, 128), BF16)],
    )
    coef = lax.all_to_all(coef, torus, 0, 0)
    both = lax.ppermute(samp, SAMP, [(i, 3 - i) for i in range(RING)])
    zhi = lax.ppermute(samp, "zhi", [(0, 1), (1, 0)])
    core = lax.ppermute(samp, "core", [(0, 1), (1, 0)])
    everyone, bias, message = small(
        join_body, "join",
        [struct((RING, 64, 128), BF16), struct((8, 128), F32), struct((16, 64, 128), BF16)],
        samp_at, samp, both, zhi, core,
    )
    coef, message = lax.optimization_barrier((coef, message))
    message = lax.all_to_all(message, torus, 0, 0)
    grad_input = finish(basis, coef, point.reshape(2, vertices, 128))
    grad_w_up, grad_w_down = small(
        weights_body, "weights", [struct((128, 512), F32), struct((512, 128), F32)],
        message, scratch=[pltpu.VMEM((128, 512), F32)],
    )
    everyone = everyone.reshape(RING, 2, 2, OWNED, 128)
    grad_modes = jnp.einsum(
        "gskc,gskd->kcd", everyone[:, :, 0], everyone[:, :, 1], preferred_element_type=F32
    )
    return (grad_input, grad_modes, grad_w_up, bias[:4].reshape(512), grad_w_down)


def solution(mesh):
    fine = Mesh(mesh.devices.reshape(2, 2, RING, RING, RING), SAMP + VERT)
    in_specs = (
        P(SAMP, VERT, None),
        P(SAMP, VERT, None),
        P(VERT, None),
        P(VERT, None, None),
        P(),
        P(),
        P(),
    )
    out_specs = (P(SAMP, VERT, None), P(VERT, None, None), P(), P(), P())
    return jax.shard_map(
        per_device, mesh=fine, in_specs=in_specs, out_specs=out_specs, check_vma=False
    )
```

```python
import functools

import jax
import jax.numpy as jnp
from jax import lax
from jax.experimental import pallas as pl
from jax.experimental.pallas import tpu as pltpu
from jax.sharding import Mesh
from jax.sharding import PartitionSpec as P

F32 = jnp.float32
BF16 = jnp.bfloat16
ROOT = 0.7978845608
CUBE = 0.044715
RING = 4
OWNED = 16
SAMP = ("zhi", "core")
VERT = ("x", "zlo", "y")
MIB = 1 << 20


def product(a, b, a_dim, b_dim):
    return lax.dot_general(a, b, (((a_dim,), (b_dim,)), ((), ())), preferred_element_type=F32)


PIECES = 8
AHEAD = 3
STEP = 2048
VMEM = pl.BlockSpec(memory_space=pltpu.VMEM)
HBM = pl.BlockSpec(memory_space=pltpu.HBM)


def project_body(basis_hbm, x_hbm, c_hbm, out, basis, x, c, total, sems):
    rows = basis.shape[0] // PIECES

    def copies(i):
        at = pl.ds(i * rows, rows)
        return [
            pltpu.make_async_copy(basis_hbm.at[at], basis.at[at], sems.at[0, i]),
            pltpu.make_async_copy(x_hbm.at[:, at], x.at[:, at], sems.at[1, i]),
            pltpu.make_async_copy(c_hbm.at[:, at], c.at[:, at], sems.at[2, i]),
        ]

    for i in range(AHEAD):
        for copy in copies(i):
            copy.start()
    for i in range(PIECES):
        for copy in copies(i):
            copy.wait()
        if i + AHEAD < PIECES:
            for copy in copies(i + AHEAD):
                copy.start()
        at = slice(i * rows, (i + 1) * rows)
        fields = jnp.concatenate([x[0, at], c[0, at], x[1, at], c[1, at]], axis=1)
        part = product(basis[at], fields, 0, 0)
        if i == 0:
            total[...] = part
        else:
            total[...] += part
    for x_at in range(RING):
        for y in range(RING):
            for z in range(RING):
                first = x_at * 256 + z * 64 + y * 16
                out[x_at * RING + y, z * 16 : (z + 1) * 16, :] = total[
                    first : first + 16, :
                ].astype(BF16)


def project(basis, inputs, cotangent):
    return pl.pallas_call(
        project_body,
        in_specs=[HBM] * 3,
        out_specs=VMEM,
        out_shape=jax.ShapeDtypeStruct((16, 64, 512), BF16),
        scratch_shapes=[
            pltpu.VMEM(basis.shape, BF16),
            pltpu.VMEM(inputs.shape, BF16),
            pltpu.VMEM(cotangent.shape, BF16),
            pltpu.VMEM((1024, 512), F32),
            pltpu.SemaphoreType.DMA((3, PIECES)),
        ],
        compiler_params=pltpu.CompilerParams(vmem_limit_bytes=56 * MIB),
        cost_estimate=pl.CostEstimate(
            flops=2 * 4096 * 1024 * 512, bytes_accessed=13 * MIB, transcendentals=0
        ),
        name="project",
    )(basis, inputs, cotangent)


def pointwise_body(
    x_hbm, c_hbm, up_ref, bias_ref, down_ref, p_hbm, out, x_ref, c_ref, p_ref, gu_ref, gd_ref, gb_ref, sems
):
    rows = STEP
    count = x_ref.shape[0] // rows

    def copy(k, i, at):
        if k == 2:
            return pltpu.make_async_copy(p_ref.at[at], p_hbm.at[at], sems.at[2, i])
        source, held = ((x_hbm, x_ref), (c_hbm, c_ref))[k]
        return pltpu.make_async_copy(source.at[at], held.at[at], sems.at[k, i])

    def load(i):
        at = pl.ds(pl.multiple_of(i * rows, rows), rows)
        copy(0, i, at).start()
        copy(1, i, at).start()

    load(0)
    gu_ref[...] = jnp.zeros_like(gu_ref)
    gd_ref[...] = jnp.zeros_like(gd_ref)
    gb_ref[...] = jnp.zeros_like(gb_ref)

    @pl.loop(0, count)
    def _(i):
        at = pl.ds(pl.multiple_of(i * rows, rows), rows)
        copy(0, i, at).wait()
        copy(1, i, at).wait()

        @pl.when(i + 1 < count)
        def _():
            load(i + 1)

        up, down = up_ref[...], down_ref[...]
        x, c = x_ref[at, :], c_ref[at, :]
        z = product(x, up, 1, 0) + bias_ref[...]
        square = z * z
        q = 0.5 + 0.5 * jnp.tanh(z * (ROOT + (ROOT * CUBE) * square))
        value = z * q
        hidden = value.astype(BF16)
        slope = q + (value - value * q) * (2.0 * ROOT + (6.0 * CUBE * ROOT) * square)
        exact = product(c, down, 1, 1) * slope
        gb_ref[...] += jnp.sum(exact.reshape(rows // 8, 8, 512), axis=0)
        grad_pre = exact.astype(BF16)
        p_ref[at, :] = product(grad_pre, up, 1, 1).astype(BF16)
        copy(2, i, at).start()
        gu_ref[...] += product(x, grad_pre, 0, 0)
        gd_ref[...] += product(c, hidden, 0, 0)

    row = lax.broadcasted_iota(jnp.int32, (8, 128), 0)
    sums = jnp.sum(gb_ref[...], axis=0, keepdims=True)
    bias = jnp.zeros((8, 128), F32)
    for g in range(4):
        bias = jnp.where(row == g, sums[:, g * 128 : (g + 1) * 128], bias)
    for j in range(16):
        tiles = [
            ref[j * 8 : (j + 1) * 8, g * 128 : (g + 1) * 128]
            for ref in (gu_ref, gd_ref)
            for g in range(4)
        ]
        out[j] = jnp.concatenate(tiles + [bias], axis=0).astype(BF16)
    for i in range(count):
        copy(2, i, pl.ds(i * rows, rows)).wait()


def pointwise(x, c, up, bias, down):
    rows = x.shape[0]
    return pl.pallas_call(
        pointwise_body,
        in_specs=[HBM, HBM] + [VMEM] * 3,
        out_specs=[HBM, VMEM],
        out_shape=[jax.ShapeDtypeStruct(s, BF16) for s in (x.shape, (16, 72, 128))],
        scratch_shapes=[
            pltpu.VMEM(x.shape, BF16),
            pltpu.VMEM(c.shape, BF16),
            pltpu.VMEM(x.shape, BF16),
            *[pltpu.VMEM(s, F32) for s in ((128, 512), (128, 512), (8, 512))],
            pltpu.SemaphoreType.DMA((3, rows // STEP)),
        ],
        compiler_params=pltpu.CompilerParams(vmem_limit_bytes=52 * MIB),
        cost_estimate=pl.CostEstimate(
            flops=10 * rows * 128 * 512, bytes_accessed=rows * 128 * 8, transcendentals=rows * 512
        ),
        name="pointwise",
    )(x, c, up, bias, down)


def small(body, name, out_shape, *args, scratch=()):
    return pl.pallas_call(
        body,
        out_shape=out_shape,
        in_specs=[
            pl.BlockSpec(memory_space=pltpu.SMEM if v.dtype == jnp.int32 else pltpu.VMEM)
            for v in args
        ],
        scratch_shapes=list(scratch),
        compiler_params=pltpu.CompilerParams(vmem_limit_bytes=32 * MIB),
        name=name,
    )(*args)


def line_body(z_at, messages, own, one, two, three, total):
    sums = messages[0].astype(F32)
    for j in range(1, 16):
        sums = sums + messages[j].astype(F32)
    total[...] = sums
    for shift, out in enumerate((own, one, two, three)):
        first = pl.multiple_of(lax.rem(z_at[0] + shift, RING) * 16, 16)
        out[...] = total[pl.ds(first, 16), :]


def own_body(own, one, two, three, weights, pieces, modes_ref, line_ref):
    total = (own[...] + two[...]) + (one[...] + three[...])
    for g in range(4):
        modes_ref[g * 16 : (g + 1) * 16, :] = total[:, g * 128 : (g + 1) * 128].astype(BF16)
    grads = pieces[0].astype(F32)
    for j in range(1, 16):
        grads = grads + pieces[j].astype(F32)
    parts = []
    for sample in range(2):
        rest = total[:, sample * 256 + 128 : sample * 256 + 256]
        for _ in range(3):
            parts.append(rest.astype(BF16))
            rest = rest - parts[-1].astype(F32)
    left = jnp.concatenate(parts, axis=0)
    row = lax.broadcasted_iota(jnp.int32, (16, 128), 0)
    first = jnp.zeros((16, 128), F32)
    second = jnp.zeros((16, 128), F32)
    for k in range(16):
        mixed = product(left, weights[k], 1, 1)
        first = jnp.where(row == k, mixed[0:16] + mixed[16:32] + mixed[32:48], first)
        second = jnp.where(row == k, mixed[48:64] + mixed[64:80] + mixed[80:96], second)
    line_ref[...] = jnp.concatenate([first, second, grads], axis=0).astype(BF16)


def gather_body(z_at, own, one, two, three, modes, coef_ref, samp_ref, held):
    for shift, ref in enumerate((own, one, two, three)):
        held[lax.rem(z_at[0] + RING - shift, RING)] = ref[0:32, :]
    coef = held[...].reshape(128, 128)
    for v in range(16):
        coef_ref[v] = coef
    parts = [ref[32:104, :].astype(F32) for ref in (own, one, two, three)]
    grads = (parts[0] + parts[2]) + (parts[1] + parts[3])
    samp_ref[0:64, :] = modes[...]
    samp_ref[64:136, :] = grads.astype(BF16)


def pair_body(at, own, core, out):
    place = lax.rem(at[0], 2)
    for k, ref in ((place, own), (1 - place, core)):
        out[pl.ds(pl.multiple_of(k * 64, 64), 64), :] = ref[0:64, :]
    grads = own[64:136, :].astype(F32) + core[64:136, :].astype(F32)
    out[128:200, :] = grads.astype(BF16)


def join_body(at, own, zhi, everyone, bias, message):
    half = lax.div(at[0], 2)
    everyone[half] = own[0:128, :]
    everyone[1 - half] = zhi[0:128, :]
    grads = own[128:200, :].astype(F32) + zhi[128:200, :].astype(F32)
    bias[...] = jnp.concatenate([grads[64 + g : 65 + g] for g in range(4)], axis=1)
    body = grads[0:64].astype(BF16)
    for v in range(16):
        message[v] = body


def finish_body(basis_ref, message_ref, p_ref, out_ref, coef):
    @pl.when(pl.program_id(0) == 0)
    def _():
        for x in range(RING):
            for y in range(RING):
                for z in range(RING):
                    first = x * 256 + z * 64 + y * 16
                    for half in range(2):
                        coef[first : first + 16, half * 128 : (half + 1) * 128] = message_ref[
                            x * RING + y, z * 32 + half * 16 : z * 32 + half * 16 + 16, :
                        ]

    total = product(basis_ref[...], coef[...], 1, 0)
    out_ref[0] = (total[:, :128] + p_ref[0].astype(F32)).astype(out_ref.dtype)
    out_ref[1] = (total[:, 128:] + p_ref[1].astype(F32)).astype(out_ref.dtype)


def finish(basis, message, point, rows=2048):
    vertices = basis.shape[0]
    both = pl.BlockSpec((2, rows, 128), lambda i: (0, i, 0))
    return pl.pallas_call(
        finish_body,
        grid=(vertices // rows,),
        in_specs=[
            pl.BlockSpec((rows, 1024), lambda i: (i, 0)),
            pl.BlockSpec(message.shape, lambda i: (0, 0, 0)),
            both,
        ],
        out_specs=both,
        out_shape=jax.ShapeDtypeStruct((2, vertices, 128), BF16),
        scratch_shapes=[pltpu.VMEM((1024, 256), BF16)],
        compiler_params=pltpu.CompilerParams(vmem_limit_bytes=56 * MIB),
        cost_estimate=pl.CostEstimate(
            flops=2 * vertices * 1024 * 256, bytes_accessed=16 * MIB, transcendentals=0
        ),
        name="finish",
    )(basis, message, point)


def weights_body(message, gu_ref, gd_ref, down):
    for j in range(16):
        tiles = message[j].astype(F32)
        for k, ref in enumerate((gu_ref, down)):
            for g in range(4):
                first = k * 32 + g * 8
                ref[j * 8 : (j + 1) * 8, g * 128 : (g + 1) * 128] = tiles[first : first + 8]
    gd_ref[...] = down[...].T


def shift(value, axis, by):
    return lax.ppermute(value, axis, [(i, (i + by) % RING) for i in range(RING)])


def per_device(inputs, cotangent, basis, mode_weights, w_up, b_up, w_down):
    z_at = lax.axis_index("zlo").reshape(1)
    samp_at = (lax.axis_index("zhi") * 2 + lax.axis_index("core")).reshape(1)
    vertices = inputs.shape[1]
    struct = jax.ShapeDtypeStruct

    packed = project(basis, inputs, cotangent)
    inputs, cotangent, packed = lax.optimization_barrier((inputs, cotangent, packed))
    messages = lax.all_to_all(packed, ("x", "y"), 0, 0)
    point, pieces = pointwise(
        inputs.reshape(-1, 128), cotangent.reshape(-1, 128), w_up, b_up.reshape(1, 512), w_down
    )
    torus = ("x", "y")
    pieces = lax.all_to_all(pieces, torus, 0, 0)
    own, *chunks = small(
        line_body, "line", [struct((16, 512), F32)] * 4,
        z_at, messages, scratch=[pltpu.VMEM((64, 512), F32)],
    )
    arrived = [shift(chunks[s - 1], "zlo", s) for s in (1, 2, 3)]
    modes, line = small(
        own_body, "own", [struct((64, 128), BF16), struct((104, 128), BF16)],
        own, *arrived, mode_weights, pieces,
    )
    coef, samp = small(
        gather_body, "gather", [struct((16, 128, 128), BF16), struct((136, 128), BF16)],
        z_at, line, *[shift(line, "zlo", s) for s in (1, 2, 3)], modes,
        scratch=[pltpu.VMEM((RING, 32, 128), BF16)],
    )
    coef = lax.all_to_all(coef, torus, 0, 0)
    core = lax.ppermute(samp, "core", [(0, 1), (1, 0)])
    pair = small(pair_body, "pair", struct((200, 128), BF16), samp_at, samp, core)
    zhi = lax.ppermute(pair, "zhi", [(0, 1), (1, 0)])
    everyone, bias, message = small(
        join_body, "join",
        [struct((2, 128, 128), BF16), struct((1, 512), F32), struct((16, 64, 128), BF16)],
        samp_at, pair, zhi,
    )
    coef, message = lax.optimization_barrier((coef, message))
    message = lax.all_to_all(message, torus, 0, 0)
    grad_input = finish(basis, coef, point.reshape(2, vertices, 128))
    grad_w_up, grad_w_down = small(
        weights_body, "weights", [struct((128, 512), F32), struct((512, 128), F32)],
        message, scratch=[pltpu.VMEM((128, 512), F32)],
    )
    everyone = everyone.reshape(RING, 2, 2, OWNED, 128)
    grad_modes = jnp.einsum(
        "gskc,gskd->kcd", everyone[:, :, 0], everyone[:, :, 1], preferred_element_type=F32
    )
    return (grad_input, grad_modes, grad_w_up, bias.reshape(512), grad_w_down)


def solution(mesh):
    fine = Mesh(mesh.devices.reshape(2, 2, RING, RING, RING), SAMP + VERT)
    in_specs = (
        P(SAMP, VERT, None),
        P(SAMP, VERT, None),
        P(VERT, None),
        P(VERT, None, None),
        P(),
        P(),
        P(),
    )
    out_specs = (P(SAMP, VERT, None), P(VERT, None, None), P(), P(), P())
    return jax.shard_map(
        per_device, mesh=fine, in_specs=in_specs, out_specs=out_specs, check_vma=False
    )
```

```python
import functools

import jax
import jax.numpy as jnp
from jax import lax
from jax.experimental import pallas as pl
from jax.experimental.pallas import tpu as pltpu
from jax.sharding import Mesh
from jax.sharding import PartitionSpec as P

F32 = jnp.float32
BF16 = jnp.bfloat16
ROOT = 0.7978845608
CUBE = 0.044715
RING = 4
OWNED = 16
SAMP = ("zhi", "core")
VERT = ("x", "zlo", "y")
MIB = 1 << 20


def product(a, b, a_dim, b_dim):
    return lax.dot_general(a, b, (((a_dim,), (b_dim,)), ((), ())), preferred_element_type=F32)


PIECES = 8
AHEAD = 3
STEP = 2048
VMEM = pl.BlockSpec(memory_space=pltpu.VMEM)
HBM = pl.BlockSpec(memory_space=pltpu.HBM)


def project_body(basis_hbm, x_hbm, c_hbm, out, basis, x, c, total, sems):
    rows = basis.shape[0] // PIECES

    def copies(i):
        at = pl.ds(i * rows, rows)
        return [
            pltpu.make_async_copy(basis_hbm.at[at], basis.at[at], sems.at[0, i]),
            pltpu.make_async_copy(x_hbm.at[:, at], x.at[:, at], sems.at[1, i]),
            pltpu.make_async_copy(c_hbm.at[:, at], c.at[:, at], sems.at[2, i]),
        ]

    for i in range(AHEAD):
        for copy in copies(i):
            copy.start()
    for i in range(PIECES):
        for copy in copies(i):
            copy.wait()
        if i + AHEAD < PIECES:
            for copy in copies(i + AHEAD):
                copy.start()
        at = slice(i * rows, (i + 1) * rows)
        fields = jnp.concatenate([x[0, at], c[0, at], x[1, at], c[1, at]], axis=1)
        part = product(basis[at], fields, 0, 0)
        if i == 0:
            total[...] = part
        else:
            total[...] += part
    for x_at in range(RING):
        for y in range(RING):
            for z in range(RING):
                first = x_at * 256 + z * 64 + y * 16
                out[x_at * RING + y, z * 16 : (z + 1) * 16, :] = total[
                    first : first + 16, :
                ].astype(BF16)


def project(basis, inputs, cotangent):
    return pl.pallas_call(
        project_body,
        in_specs=[HBM] * 3,
        out_specs=VMEM,
        out_shape=jax.ShapeDtypeStruct((16, 64, 512), BF16),
        scratch_shapes=[
            pltpu.VMEM(basis.shape, BF16),
            pltpu.VMEM(inputs.shape, BF16),
            pltpu.VMEM(cotangent.shape, BF16),
            pltpu.VMEM((1024, 512), F32),
            pltpu.SemaphoreType.DMA((3, PIECES)),
        ],
        compiler_params=pltpu.CompilerParams(vmem_limit_bytes=56 * MIB),
        cost_estimate=pl.CostEstimate(
            flops=2 * 4096 * 1024 * 512, bytes_accessed=13 * MIB, transcendentals=0
        ),
        name="project",
    )(basis, inputs, cotangent)


def pointwise_body(
    x_hbm, c_hbm, up_ref, bias_ref, down_ref, p_hbm, out, x_ref, c_ref, p_ref, gu_ref, gd_ref, gb_ref, sems
):
    rows = STEP
    count = x_ref.shape[0] // rows

    def copy(k, i, at):
        if k == 2:
            return pltpu.make_async_copy(p_ref.at[at], p_hbm.at[at], sems.at[2, i])
        source, held = ((x_hbm, x_ref), (c_hbm, c_ref))[k]
        return pltpu.make_async_copy(source.at[at], held.at[at], sems.at[k, i])

    def load(i):
        at = pl.ds(pl.multiple_of(i * rows, rows), rows)
        copy(0, i, at).start()
        copy(1, i, at).start()

    load(0)
    gu_ref[...] = jnp.zeros_like(gu_ref)
    gd_ref[...] = jnp.zeros_like(gd_ref)
    gb_ref[...] = jnp.zeros_like(gb_ref)

    @pl.loop(0, count)
    def _(i):
        at = pl.ds(pl.multiple_of(i * rows, rows), rows)
        copy(0, i, at).wait()
        copy(1, i, at).wait()

        @pl.when(i + 1 < count)
        def _():
            load(i + 1)

        up, down = up_ref[...], down_ref[...]
        x, c = x_ref[at, :], c_ref[at, :]
        z = product(x, up, 1, 0) + bias_ref[...]
        square = z * z
        q = 0.5 + 0.5 * jnp.tanh(z * (ROOT + (ROOT * CUBE) * square))
        value = z * q
        hidden = value.astype(BF16)
        slope = q + (value - value * q) * (2.0 * ROOT + (6.0 * CUBE * ROOT) * square)
        exact = product(c, down, 1, 1) * slope
        gb_ref[...] += jnp.sum(exact.reshape(rows // 8, 8, 512), axis=0)
        grad_pre = exact.astype(BF16)
        p_ref[at, :] = product(grad_pre, up, 1, 1).astype(BF16)
        copy(2, i, at).start()
        gu_ref[...] += product(x, grad_pre, 0, 0)
        gd_ref[...] += product(c, hidden, 0, 0)

    row = lax.broadcasted_iota(jnp.int32, (8, 128), 0)
    sums = jnp.sum(gb_ref[...], axis=0, keepdims=True)
    bias = jnp.zeros((8, 128), F32)
    for g in range(4):
        bias = jnp.where(row == g, sums[:, g * 128 : (g + 1) * 128], bias)
    for j in range(16):
        tiles = [
            ref[j * 8 : (j + 1) * 8, g * 128 : (g + 1) * 128]
            for ref in (gu_ref, gd_ref)
            for g in range(4)
        ]
        out[j] = jnp.concatenate(tiles + [bias], axis=0).astype(BF16)
    for i in range(count):
        copy(2, i, pl.ds(i * rows, rows)).wait()


def pointwise(x, c, up, bias, down):
    rows = x.shape[0]
    return pl.pallas_call(
        pointwise_body,
        in_specs=[HBM, HBM] + [VMEM] * 3,
        out_specs=[HBM, VMEM],
        out_shape=[jax.ShapeDtypeStruct(s, BF16) for s in (x.shape, (16, 72, 128))],
        scratch_shapes=[
            pltpu.VMEM(x.shape, BF16),
            pltpu.VMEM(c.shape, BF16),
            pltpu.VMEM(x.shape, BF16),
            *[pltpu.VMEM(s, F32) for s in ((128, 512), (128, 512), (8, 512))],
            pltpu.SemaphoreType.DMA((3, rows // STEP)),
        ],
        compiler_params=pltpu.CompilerParams(vmem_limit_bytes=52 * MIB),
        cost_estimate=pl.CostEstimate(
            flops=10 * rows * 128 * 512, bytes_accessed=rows * 128 * 8, transcendentals=rows * 512
        ),
        name="pointwise",
    )(x, c, up, bias, down)


def small(body, name, out_shape, *args, scratch=()):
    return pl.pallas_call(
        body,
        out_shape=out_shape,
        in_specs=[
            pl.BlockSpec(memory_space=pltpu.SMEM if v.dtype == jnp.int32 else pltpu.VMEM)
            for v in args
        ],
        scratch_shapes=list(scratch),
        compiler_params=pltpu.CompilerParams(vmem_limit_bytes=32 * MIB),
        name=name,
    )(*args)


def line_body(z_at, messages, own, one, two, three, total):
    sums = messages[0].astype(F32)
    for j in range(1, 16):
        sums = sums + messages[j].astype(F32)
    total[...] = sums
    for shift, out in enumerate((own, one, two, three)):
        first = pl.multiple_of(lax.rem(z_at[0] + shift, RING) * 16, 16)
        out[...] = total[pl.ds(first, 16), :].astype(out.dtype)


def own_body(own, one, two, three, weights, pieces, modes_ref, line_ref):
    total = (own[...] + two[...].astype(F32)) + (one[...].astype(F32) + three[...].astype(F32))
    for g in range(4):
        modes_ref[g * 16 : (g + 1) * 16, :] = total[:, g * 128 : (g + 1) * 128].astype(BF16)
    grads = pieces[0].astype(F32)
    for j in range(1, 16):
        grads = grads + pieces[j].astype(F32)
    parts = []
    for sample in range(2):
        rest = total[:, sample * 256 + 128 : sample * 256 + 256]
        for _ in range(3):
            parts.append(rest.astype(BF16))
            rest = rest - parts[-1].astype(F32)
    left = jnp.concatenate(parts, axis=0)
    row = lax.broadcasted_iota(jnp.int32, (16, 128), 0)
    first = jnp.zeros((16, 128), F32)
    second = jnp.zeros((16, 128), F32)
    for k in range(16):
        mixed = product(left, weights[k], 1, 1)
        first = jnp.where(row == k, mixed[0:16] + mixed[16:32] + mixed[32:48], first)
        second = jnp.where(row == k, mixed[48:64] + mixed[64:80] + mixed[80:96], second)
    line_ref[...] = jnp.concatenate([first, second, grads], axis=0).astype(BF16)


def gather_body(z_at, own, one, two, three, modes, coef_ref, samp_ref, held):
    for shift, ref in enumerate((own, one, two, three)):
        held[lax.rem(z_at[0] + RING - shift, RING)] = ref[0:32, :]
    coef = held[...].reshape(128, 128)
    for v in range(16):
        coef_ref[v] = coef
    parts = [ref[32:104, :].astype(F32) for ref in (own, one, two, three)]
    grads = (parts[0] + parts[2]) + (parts[1] + parts[3])
    samp_ref[0:64, :] = modes[...]
    samp_ref[64:136, :] = grads.astype(BF16)


def pair_body(at, own, core, out):
    place = lax.rem(at[0], 2)
    for k, ref in ((place, own), (1 - place, core)):
        out[pl.ds(pl.multiple_of(k * 64, 64), 64), :] = ref[0:64, :]
    grads = own[64:136, :].astype(F32) + core[64:136, :].astype(F32)
    out[128:200, :] = grads.astype(BF16)


def join_body(at, own, zhi, everyone, bias, message):
    half = lax.div(at[0], 2)
    everyone[half] = own[0:128, :]
    everyone[1 - half] = zhi[0:128, :]
    grads = own[128:200, :].astype(F32) + zhi[128:200, :].astype(F32)
    bias[...] = jnp.concatenate([grads[64 + g : 65 + g] for g in range(4)], axis=1)
    body = grads[0:64].astype(BF16)
    for v in range(16):
        message[v] = body


def finish_body(basis_ref, message_ref, p_ref, out_ref, coef):
    @pl.when(pl.program_id(0) == 0)
    def _():
        for x in range(RING):
            for y in range(RING):
                for z in range(RING):
                    first = x * 256 + z * 64 + y * 16
                    for half in range(2):
                        coef[first : first + 16, half * 128 : (half + 1) * 128] = message_ref[
                            x * RING + y, z * 32 + half * 16 : z * 32 + half * 16 + 16, :
                        ]

    total = product(basis_ref[...], coef[...], 1, 0)
    out_ref[0] = (total[:, :128] + p_ref[0].astype(F32)).astype(out_ref.dtype)
    out_ref[1] = (total[:, 128:] + p_ref[1].astype(F32)).astype(out_ref.dtype)


def finish(basis, message, point, rows=2048):
    vertices = basis.shape[0]
    both = pl.BlockSpec((2, rows, 128), lambda i: (0, i, 0))
    return pl.pallas_call(
        finish_body,
        grid=(vertices // rows,),
        in_specs=[
            pl.BlockSpec((rows, 1024), lambda i: (i, 0)),
            pl.BlockSpec(message.shape, lambda i: (0, 0, 0)),
            both,
        ],
        out_specs=both,
        out_shape=jax.ShapeDtypeStruct((2, vertices, 128), BF16),
        scratch_shapes=[pltpu.VMEM((1024, 256), BF16)],
        compiler_params=pltpu.CompilerParams(vmem_limit_bytes=56 * MIB),
        cost_estimate=pl.CostEstimate(
            flops=2 * vertices * 1024 * 256, bytes_accessed=16 * MIB, transcendentals=0
        ),
        name="finish",
    )(basis, message, point)


def weights_body(message, gu_ref, gd_ref, down):
    for j in range(16):
        tiles = message[j].astype(F32)
        for k, ref in enumerate((gu_ref, down)):
            for g in range(4):
                first = k * 32 + g * 8
                ref[j * 8 : (j + 1) * 8, g * 128 : (g + 1) * 128] = tiles[first : first + 8]
    gd_ref[...] = down[...].T


def shift(value, axis, by):
    return lax.ppermute(value, axis, [(i, (i + by) % RING) for i in range(RING)])


def per_device(inputs, cotangent, basis, mode_weights, w_up, b_up, w_down):
    z_at = lax.axis_index("zlo").reshape(1)
    samp_at = (lax.axis_index("zhi") * 2 + lax.axis_index("core")).reshape(1)
    vertices = inputs.shape[1]
    struct = jax.ShapeDtypeStruct

    packed = project(basis, inputs, cotangent)
    inputs, cotangent, packed = lax.optimization_barrier((inputs, cotangent, packed))
    messages = lax.all_to_all(packed, ("x", "y"), 0, 0)
    point, pieces = pointwise(
        inputs.reshape(-1, 128), cotangent.reshape(-1, 128), w_up, b_up.reshape(1, 512), w_down
    )
    torus = ("x", "y")
    pieces = lax.all_to_all(pieces, torus, 0, 0)
    own, *chunks = small(
        line_body, "line", [struct((16, 512), F32)] + [struct((16, 512), BF16)] * 3,
        z_at, messages, scratch=[pltpu.VMEM((64, 512), F32)],
    )
    arrived = [shift(chunks[s - 1], "zlo", s) for s in (1, 2, 3)]
    modes, line = small(
        own_body, "own", [struct((64, 128), BF16), struct((104, 128), BF16)],
        own, *arrived, mode_weights, pieces,
    )
    coef, samp = small(
        gather_body, "gather", [struct((16, 128, 128), BF16), struct((136, 128), BF16)],
        z_at, line, *[shift(line, "zlo", s) for s in (1, 2, 3)], modes,
        scratch=[pltpu.VMEM((RING, 32, 128), BF16)],
    )
    coef = lax.all_to_all(coef, torus, 0, 0)
    core = lax.ppermute(samp, "core", [(0, 1), (1, 0)])
    pair = small(pair_body, "pair", struct((200, 128), BF16), samp_at, samp, core)
    zhi = lax.ppermute(pair, "zhi", [(0, 1), (1, 0)])
    everyone, bias, message = small(
        join_body, "join",
        [struct((2, 128, 128), BF16), struct((1, 512), F32), struct((16, 64, 128), BF16)],
        samp_at, pair, zhi,
    )
    coef, message = lax.optimization_barrier((coef, message))
    message = lax.all_to_all(message, torus, 0, 0)
    grad_input = finish(basis, coef, point.reshape(2, vertices, 128))
    grad_w_up, grad_w_down = small(
        weights_body, "weights", [struct((128, 512), F32), struct((512, 128), F32)],
        message, scratch=[pltpu.VMEM((128, 512), F32)],
    )
    everyone = everyone.reshape(RING, 2, 2, OWNED, 128)
    grad_modes = jnp.einsum(
        "gskc,gskd->kcd", everyone[:, :, 0], everyone[:, :, 1], preferred_element_type=F32
    )
    return (grad_input, grad_modes, grad_w_up, bias.reshape(512), grad_w_down)


def solution(mesh):
    fine = Mesh(mesh.devices.reshape(2, 2, RING, RING, RING), SAMP + VERT)
    in_specs = (
        P(SAMP, VERT, None),
        P(SAMP, VERT, None),
        P(VERT, None),
        P(VERT, None, None),
        P(),
        P(),
        P(),
    )
    out_specs = (P(SAMP, VERT, None), P(VERT, None, None), P(), P(), P())
    return jax.shard_map(
        per_device, mesh=fine, in_specs=in_specs, out_specs=out_specs, check_vma=False
    )
```
